32 devices in a mesh: occ: 8 (over z, y), aux: 4 (over x, core).
Axes of the slice: x: 2, y: 2, z: 4, core: 2. Of those that a mesh axis runs over, the one named last changes fastest.
Arguments:
- b_alpha: bfloat16 [16, 512, 1536], P('occ', None, 'aux'), may hold values from -0.95703125 to 0.95703125
- b_beta: bfloat16 [16, 512, 1536], P('occ', None, 'aux'), may hold values from -0.95703125 to 0.95703125
- eps_occ_alpha: float32 [16], replicated, may hold values from -3 to -0.3
- eps_occ_beta: float32 [16], replicated, may hold values from -3 to -0.3
- eps_vir_alpha: float32 [512], replicated, may hold values from 0.2 to 4
- eps_vir_beta: float32 [512], replicated, may hold values from 0.2 to 4
- row_orbital: int32 [16], replicated, may hold values from 0 to 15, as said below
- pair_list: int32 [4, 8, 2], replicated, may hold values from 0 to 15, as said below
- live_mask: int32 [4, 8], replicated, may hold values 0 or 1
Outputs:
- gamma_alpha: float32 [16, 512, 1536], P('occ', None, 'aux')
- gamma_beta: float32 [16, 512, 1536], P('occ', None, 'aux')
The draws below stay inside these ranges and needn't reach their ends.
Inputs may be any that keep to these rules, and one draw needn't show every extreme that they name: A permutation: stored row r of b_alpha, b_beta and the outputs belongs to occupied orbital row_orbital[r]. `pair_list`: for slot s and worker w the entry (i, j) has r(i) among the stored rows w * 2 to (w + 1) * 2 - 1 and r(j) among the stored rows of worker (w - d) mod 8, where d = 1 + s * (8 // 4) and r is the inverse of row_orbital.
All inputs are finite; a program needn't handle non-finite values.
Results may differ from the reference program's by a relative error of at most 0.01.
Values may be sent and summed in bfloat16 or wider, within the bound.
A program may use at most 64 MiB of HBM per device.

```python
import jax
import jax.numpy as jnp
from jax import lax

NVIR = 512
NAUX = 1536
OCC_DEV = 2
BATCHES = 2
ROUNDS = 2
OCC = 16
SLOTS = 4
N_OCC = 8
N_AUX = 4


def orbital_map(key):
    return jax.random.permutation(jax.random.fold_in(key, 11), OCC).astype(jnp.int32)


def draw_row_orbital(key, part):
    return orbital_map(key)


def draw_pair_list(key, part):
    mapping = orbital_map(key)
    workers = OCC // OCC_DEV
    slot_count = BATCHES * ROUNDS
    distances = 1 + jnp.arange(slot_count, dtype=jnp.int32) * (workers // slot_count)
    owners = jnp.arange(workers, dtype=jnp.int32)
    pick_i = jax.random.randint(jax.random.fold_in(key, 23), (slot_count, workers), 0, OCC_DEV)
    pick_j = jax.random.randint(jax.random.fold_in(key, 29), (slot_count, workers), 0, OCC_DEV)
    rows_i = owners[None, :] * OCC_DEV + pick_i
    rows_j = jnp.mod(owners[None, :] - distances[:, None], workers) * OCC_DEV + pick_j
    return jnp.stack([mapping[rows_i], mapping[rows_j]], axis=-1).astype(jnp.int32)


def plant(values, stream_key, smallest, top_value):
    place = [jax.random.randint(jax.random.fold_in(stream_key, axis), (), 0, length) for axis, length in enumerate(values.shape)]
    widest = values.shape.index(max(values.shape))
    next_to = place[:widest] + [(place[widest] + 1) % values.shape[widest]] + place[widest + 1:]
    return values.at[tuple(place)].set(smallest).at[tuple(next_to)].set(top_value)


def level_of(own_key, extent, cuts, least, largest):
    gain, own = 1.0, jax.random.fold_in(own_key, 6)
    for dim, shards_of in cuts:
        draws = jnp.exp(jax.random.uniform(jax.random.fold_in(own, dim), (shards_of,), jnp.float32, least / len(cuts), largest / len(cuts)))
        gain = gain * jnp.repeat(draws, extent[dim] // shards_of).reshape([-1 if axis == dim else 1 for axis in range(len(extent))])
    return gain


def noise(rng, shape, spread, bound, shards=(), kind=jnp.bfloat16):
    level = level_of(rng, shape, shards, -0.22, 0.18) if shards else 1.0
    drawn = jax.random.normal(rng, shape, jnp.float32) * spread * level
    return jnp.minimum(jnp.maximum(drawn, -bound), bound).astype(kind)


def setup_inputs(seed: int = 0) -> dict:
    streams_of = jax.random.split(jax.random.key(seed), 10)
    b_alpha = noise(streams_of[0], (OCC, NVIR, NAUX), 0.16, 0.95703125, ((0, 8), (2, 4)))
    b_beta = noise(streams_of[1], (OCC, NVIR, NAUX), 0.16, 0.95703125, ((0, 8), (2, 4)))
    eps_occ_alpha = jnp.clip(jax.random.uniform(streams_of[2], (OCC,), jnp.float32, -3.0, -0.3), -3.0, -0.3)
    eps_occ_beta = jnp.clip(jax.random.uniform(streams_of[3], (OCC,), jnp.float32, -3.0, -0.3), -3.0, -0.3)
    eps_vir_alpha = jnp.clip(jax.random.uniform(streams_of[4], (NVIR,), jnp.float32, 0.2, 4.0), 0.2, 4.0)
    eps_vir_beta = jnp.clip(jax.random.uniform(streams_of[5], (NVIR,), jnp.float32, 0.2, 4.0), 0.2, 4.0)
    row_orbital = draw_row_orbital(jax.random.fold_in(streams_of[9], 71), 0)
    pair_list = draw_pair_list(jax.random.fold_in(streams_of[9], 71), 0)
    live_mask = plant((jax.random.randint(streams_of[8], (SLOTS, N_OCC), 0, 4) < 3).astype(jnp.int32), jax.random.fold_in(streams_of[8], 1), 0, 1)
    return {"b_alpha": b_alpha, "b_beta": b_beta, "eps_occ_alpha": eps_occ_alpha, "eps_occ_beta": eps_occ_beta, "eps_vir_alpha": eps_vir_alpha, "eps_vir_beta": eps_vir_beta, "row_orbital": row_orbital, "pair_list": pair_list, "live_mask": live_mask}


def add_row(totals, row_index, row_term):
    current = lax.dynamic_index_in_dim(totals, row_index, 0, keepdims=False)
    return lax.dynamic_update_index_in_dim(totals, current + row_term, row_index, 0)


def reference(b_alpha, b_beta, eps_occ_alpha, eps_occ_beta, eps_vir_alpha, eps_vir_beta, row_orbital, pair_list, live_mask):
    places = jnp.arange(OCC, dtype=jnp.int32)
    inverse = jnp.zeros((OCC,), jnp.int32).at[row_orbital].set(places)
    alpha_full = b_alpha.astype(jnp.float32)
    beta_full = b_beta.astype(jnp.float32)
    flat_pairs = pair_list.reshape(-1, 2).astype(jnp.int32)
    flat_live = live_mask.reshape(-1).astype(jnp.float32)

    def advance(state_pair, item):
        gamma_alpha, gamma_beta = state_pair
        orbitals, live_flag = item
        row_i = inverse[orbitals[0]].astype(jnp.int32)
        row_j = inverse[orbitals[1]].astype(jnp.int32)
        block_i = lax.dynamic_index_in_dim(alpha_full, row_i, 0, keepdims=False)
        block_j = lax.dynamic_index_in_dim(beta_full, row_j, 0, keepdims=False)
        split_i = block_i.reshape(NVIR, N_AUX, NAUX // N_AUX)
        split_j = block_j.reshape(NVIR, N_AUX, NAUX // N_AUX)
        partials = jnp.einsum("akp,bkp->kab", split_i, split_j, precision=lax.Precision.HIGHEST)
        rounded = lax.optimization_barrier(partials.astype(jnp.bfloat16))
        integrals = jnp.sum(rounded.astype(jnp.float32), axis=0)
        energy_gap = eps_vir_alpha[:, None] + eps_vir_beta[None, :] - eps_occ_alpha[orbitals[0]] - eps_occ_beta[orbitals[1]]
        amplitude = (live_flag * integrals / energy_gap).astype(jnp.bfloat16)
        amplitude = lax.optimization_barrier(amplitude).astype(jnp.float32)
        term_alpha = jnp.dot(amplitude, block_j, precision=lax.Precision.HIGHEST)
        term_beta = jnp.dot(amplitude.T, block_i, precision=lax.Precision.HIGHEST)
        gamma_alpha = add_row(gamma_alpha, row_i, term_alpha)
        gamma_beta = add_row(gamma_beta, row_j, term_beta)
        return (gamma_alpha, gamma_beta), jnp.float32(0.0)

    zeros_full = jnp.zeros((OCC, NVIR, NAUX), jnp.float32)
    finals, unused = lax.scan(advance, (zeros_full, zeros_full), (flat_pairs, flat_live))
    return finals[0], finals[1]
```

```python
import functools

import jax
import jax.numpy as jnp
from jax import lax
from jax.experimental import pallas as pl
from jax.experimental.pallas import tpu as pltpu
from jax.sharding import PartitionSpec as P

MESH = pl.DeviceIdType.MESH


def kernel(
    workers,
    parts,
    slots,
    chunks,
    moved,
    b_alpha_hbm,
    b_beta_hbm,
    vir_alpha_hbm,
    vir_beta_hbm,
    occ_alpha_hbm,
    occ_beta_hbm,
    row_orbital_hbm,
    pair_list_hbm,
    live_mask_hbm,
    gamma_alpha,
    gamma_beta,
    b_alpha,
    b_beta,
    eps_vir_alpha,
    eps_vir_beta,
    eps_occ_alpha,
    eps_occ_beta,
    row_orbital,
    pair_list,
    live_mask,
    send_block,
    block_j,
    half_send,
    half_recv,
    cross_send,
    cross_recv,
    amp,
    term_send,
    term_recv,
    sum_send,
    sum_recv,
    in_sems,
    fetch_sems,
    half_sems,
    cross_sems,
    pair_sems,
    far_sems,
    forward_sems,
    term_sems,
    alpha_sems,
    sum_sems,
):
    rows, nvir, cols = b_alpha.shape
    chips = parts // 2
    quarter = nvir // parts
    width = nvir // chunks
    worker = lax.axis_index("occ")
    me = lax.axis_index("aux")
    chip, core = me // 2, lax.rem(me, 2)
    partner = me + 1 - 2 * core
    odd = lax.rem(worker, 2)
    turn = 1 - 2 * odd if moved else 0
    stride = workers // slots
    distances = [k * stride + (0 if moved else 1) for k in range(slots)]
    ahead = [lax.rem(worker + d, workers) for d in distances]
    behind = [lax.rem(worker + workers - d, workers) for d in distances]
    slot = [lax.rem(k + slots - odd, slots) if moved else k for k in range(slots)]
    owner = worker + turn
    others = [lax.rem(chip + k, chips) for k in range(1, chips)]
    sources = [lax.rem(chip + chips - k, chips) for k in range(1, chips)]

    each = range(slots)
    local = 1 if moved else 0
    away = range(local, slots)
    hops = range(chips - 1)
    steps = range(chunks)
    spans = [pl.ds(c * width, width) for c in steps]

    loads = [
        pltpu.make_async_copy(src, dst, in_sems.at[n])
        for n, (src, dst) in enumerate(
            [
                (b_beta_hbm, b_beta),
                (row_orbital_hbm, row_orbital),
                (pair_list_hbm, pair_list),
                (live_mask_hbm, live_mask),
                (occ_alpha_hbm, eps_occ_alpha),
                (occ_beta_hbm, eps_occ_beta),
                (vir_alpha_hbm, eps_vir_alpha),
                (vir_beta_hbm, eps_vir_beta),
            ]
            + ([] if moved else [(b_alpha_hbm, b_alpha)])
        )
    ]
    for load in loads:
        load.start()
    barrier = pltpu.get_barrier_semaphore()
    greeted = [ahead[k] for k in away] + [behind[k] for k in away] + ([owner] if moved else [])
    for target in greeted:
        pl.semaphore_signal(barrier, inc=1, device_id={"occ": target}, device_id_type=MESH)
    for peer in [partner] + [other * 2 + core for other in others]:
        pl.semaphore_signal(barrier, inc=1, device_id={"aux": peer}, device_id_type=MESH)
    for load in loads[:3]:
        load.wait()

    def local_row(holder, label):
        found = jnp.int32(0)
        for r in range(rows):
            found = jnp.where(row_orbital[holder * rows + r] == label, r, found)
        return found

    row_i = [local_row(owner, pair_list[slot[k], 0, owner]) for k in each]
    row_out = [local_row(worker, pair_list[slot[k], 1, ahead[k] + turn]) for k in each]

    def remote(src, dst, sems, index, where):
        return pltpu.make_async_remote_copy(
            src_ref=src,
            dst_ref=dst,
            send_sem=sems.at[(0,) + index],
            recv_sem=sems.at[(1,) + index],
            device_id=where,
            device_id_type=MESH,
        )

    alphas = [
        remote(b_alpha_hbm.at[r], b_alpha.at[r], alpha_sems, (r,), {"occ": owner})
        for r in range(rows if moved else 0)
    ]
    fetches = [
        {
            k: remote(
                send_block.at[k - local, spans[c]], block_j.at[k, spans[c]], fetch_sems,
                (c, k - local), {"occ": ahead[k]},
            )
            for k in away
        }
        for c in steps
    ]
    halves = [
        remote(half_send.at[c, 1 - core], half_recv.at[c], half_sems, (c,), {"aux": partner})
        for c in steps
    ]
    crosses = [
        [
            remote(
                cross_send.at[c, k], cross_recv.at[c, k], cross_sems, (c, k),
                {"aux": others[k] * 2 + core},
            )
            for k in hops
        ]
        for c in steps
    ]
    nears = [
        remote(amp.at[c, core, chip], amp.at[c, core, chip], pair_sems, (c,), {"aux": partner})
        for c in steps
    ]
    fars = [
        [
            remote(
                amp.at[c, core, chip], amp.at[c, core, chip], far_sems, (c, k),
                {"aux": others[k] * 2 + core},
            )
            for k in hops
        ]
        for c in steps
    ]
    forwards = [
        [
            remote(
                amp.at[c, core, sources[k]], amp.at[c, core, sources[k]], forward_sems, (c, k),
                {"aux": partner},
            )
            for k in hops
        ]
        for c in steps
    ]
    returns = [
        {
            k: remote(
                term_send.at[k - local, spans[c]], term_recv.at[k - local, spans[c]], term_sems,
                (c, k - local), {"occ": behind[k]},
            )
            for k in away
        }
        for c in steps
    ]
    bands = [pl.ds(n * quarter, quarter) for n in range(parts)]
    sends = [
        remote(sum_send.at[:, bands[n]], sum_recv.at[:, bands[n]], sum_sems, (n,), {"occ": owner})
        for n in range(parts if moved else 0)
    ]

    for k in away:
        send_block[k - local, spans[0]] = b_beta[row_out[k], spans[0]]
    pl.semaphore_wait(barrier, len(greeted) + chips)
    for k in away:
        fetches[0][k].start()
    for copy in alphas:
        copy.start()
    for c in steps[1:]:
        for k in away:
            send_block[k - local, spans[c]] = b_beta[row_out[k], spans[c]]
            fetches[c][k].start()
    for k in range(local):
        block_j[k] = b_beta[row_out[k]]
    for load in loads[3:]:
        load.wait()

    vir_row = eps_vir_alpha[pl.ds(core * chips + chip, 1), :]
    vir_column = jnp.broadcast_to(vir_row, (quarter, quarter)).T[:, :1]
    for copy in alphas:
        copy.wait_recv()

    def sums(c):
        for k in each:
            if k in away:
                fetches[c][k].wait_recv()
            partial = lax.dot_general(
                b_alpha[row_i[k]],
                block_j[k, spans[c]],
                (((1,), (1,)), ((), ())),
                preferred_element_type=jnp.float32,
            )
            half_send[c, :, :, k] = partial.astype(jnp.bfloat16).reshape(2, chips, quarter, width)
        halves[c].start()

    def pair_sum(c, part):
        return half_send[c, core, part].astype(jnp.float32) + half_recv[c, part].astype(jnp.float32)

    def crossing(c):
        halves[c].wait_recv()
        for k in hops:
            cross_send[c, k] = pair_sum(c, others[k]).astype(jnp.bfloat16)
            crosses[c][k].start()

    def amplitude(c):
        total = pair_sum(c, chip)
        for k in hops:
            crosses[c][k].wait_recv()
            total = total + cross_recv[c, k].astype(jnp.float32)
        gap = vir_column + eps_vir_beta[:, spans[c]]
        for k in each:
            occ_alpha = eps_occ_alpha[pair_list[slot[k], 0, owner]]
            occ_beta = eps_occ_beta[pair_list[slot[k], 1, owner]]
            live = live_mask[slot[k], owner].astype(jnp.float32)
            value = live * total[k] / (gap - occ_alpha - occ_beta)
            amp[c, core, chip, k] = value.astype(jnp.bfloat16)
        for copy in fars[c]:
            copy.start()
        nears[c].start()

    def forward(c):
        for k in hops:
            fars[c][k].wait_recv()
            forwards[c][k].start()

    def terms(c):
        nears[c].wait_recv()
        for copy in forwards[c]:
            copy.wait_recv()
        for k in list(away) + list(range(local)):
            term = lax.dot_general(
                amp[c, :, :, k].reshape(nvir, width),
                b_alpha[row_i[k]],
                (((0,), (0,)), ((), ())),
                preferred_element_type=jnp.float32,
            )
            if k in away:
                term_send[k - local, spans[c]] = term.astype(jnp.bfloat16)
                returns[c][k].start()
            else:
                for r in range(rows):
                    gamma_beta[r, spans[c]] = jnp.where(row_out[k] == r, term, 0.0)

    for c in steps:
        sums(c)
        if c >= 1:
            forward(c - 1)
        crossing(c)
        if c >= 1:
            terms(c - 1)
        amplitude(c)
    forward(chunks - 1)
    terms(chunks - 1)
    for n in range(parts):
        totals = [jnp.zeros((quarter, cols), jnp.float32)] * rows
        for k in each:
            band = jnp.concatenate([amp[c, n // chips, n % chips, k] for c in steps], axis=1)
            term = jnp.dot(band, block_j[k], preferred_element_type=jnp.float32)
            totals = [totals[r] + jnp.where(row_i[k] == r, term, 0.0) for r in range(rows)]
        for r in range(rows):
            if moved:
                sum_send[r, bands[n]] = totals[r].astype(jnp.bfloat16)
            else:
                gamma_alpha[r, bands[n]] = totals[r]
        if moved:
            sends[n].start()
    for n, copy in enumerate(sends):
        copy.wait_recv()
        gamma_alpha[:, bands[n]] = sum_recv[:, bands[n]].astype(jnp.float32)
    for c in steps:
        for k in away:
            returns[c][k].wait_recv()
        for r in range(rows):
            total = gamma_beta[r, spans[c]] if local else jnp.zeros((width, cols), jnp.float32)
            for k in away:
                total = total + jnp.where(
                    row_out[k] == r, term_recv[k - local, spans[c]].astype(jnp.float32), 0.0
                )
            gamma_beta[r, spans[c]] = total
    for copy in alphas + sends:
        copy.wait_send()
    for c in steps:
        for copy in [fetches[c][k] for k in away] + [returns[c][k] for k in away]:
            copy.wait_send()
        for copy in [halves[c], nears[c]] + crosses[c] + fars[c] + forwards[c]:
            copy.wait_send()


def solution(mesh):
    workers, parts = mesh.shape["occ"], mesh.shape["aux"]

    def shards(
        b_alpha,
        b_beta,
        eps_occ_alpha,
        eps_occ_beta,
        eps_vir_alpha,
        eps_vir_beta,
        row_orbital,
        pair_list,
        live_mask,
    ):
        rows, nvir, cols = b_alpha.shape
        slots = pair_list.shape[0]
        quarter = nvir // parts
        chips = parts // 2
        vmem = pl.BlockSpec(memory_space=pltpu.VMEM)
        hbm = pl.BlockSpec(memory_space=pltpu.HBM)
        gamma = jax.ShapeDtypeStruct((rows, nvir, cols), jnp.float32)
        moved = workers == 2 * slots
        remote_slots = slots - 1 if moved else slots
        block = pltpu.VMEM((slots, nvir, cols), jnp.bfloat16)
        sent = pltpu.VMEM((remote_slots, nvir, cols), jnp.bfloat16)
        totals = pltpu.VMEM(b_alpha.shape, jnp.bfloat16)
        chunks = max(1, nvir // 128)
        piece = (slots, quarter, nvir // chunks)
        block_copies = pltpu.SemaphoreType.DMA((2, chunks, remote_slots))
        copies = pltpu.SemaphoreType.DMA((2, chunks))
        hop_copies = pltpu.SemaphoreType.DMA((2, chunks, chips - 1))
        pairs = jnp.transpose(pair_list, (0, 2, 1))
        return pl.pallas_call(
            functools.partial(kernel, workers, parts, slots, chunks, moved),
            out_shape=(gamma, gamma),
            in_specs=[hbm] * 9,
            out_specs=(vmem, vmem),
            scratch_shapes=[
                pltpu.VMEM(b_alpha.shape, b_alpha.dtype),
                pltpu.VMEM(b_beta.shape, b_beta.dtype),
                pltpu.VMEM((parts, quarter), jnp.float32),
                pltpu.VMEM((1, nvir), jnp.float32),
                pltpu.SMEM(eps_occ_alpha.shape, jnp.float32),
                pltpu.SMEM(eps_occ_beta.shape, jnp.float32),
                pltpu.SMEM(row_orbital.shape, jnp.int32),
                pltpu.SMEM(pairs.shape, jnp.int32),
                pltpu.SMEM(live_mask.shape, jnp.int32),
                sent,
                block,
                pltpu.VMEM((chunks, 2, chips) + piece, jnp.bfloat16),
                pltpu.VMEM((chunks, chips) + piece, jnp.bfloat16),
                pltpu.VMEM((chunks, chips - 1) + piece, jnp.bfloat16),
                pltpu.VMEM((chunks, chips - 1) + piece, jnp.bfloat16),
                pltpu.VMEM((chunks, 2, chips) + piece, jnp.bfloat16),
                sent,
                sent,
                totals,
                totals,
                pltpu.SemaphoreType.DMA((9,)),
                block_copies,
                copies,
                hop_copies,
                copies,
                hop_copies,
                hop_copies,
                block_copies,
                pltpu.SemaphoreType.DMA((2, rows)),
                pltpu.SemaphoreType.DMA((2, parts)),
            ],
            compiler_params=pltpu.CompilerParams(
                collective_id=0, has_side_effects=True, vmem_limit_bytes=56 * 1024 * 1024
            ),
        )(
            b_alpha,
            b_beta,
            eps_vir_alpha.reshape(parts, quarter),
            eps_vir_beta.reshape(1, nvir),
            eps_occ_alpha,
            eps_occ_beta,
            row_orbital,
            pairs,
            live_mask,
        )

    placed = (P("occ", None, "aux"), P("occ", None, "aux"), P(), P(), P(), P(), P(), P(), P())
    return jax.shard_map(
        shards,
        mesh=mesh,
        in_specs=placed,
        out_specs=(P("occ", None, "aux"), P("occ", None, "aux")),
        check_vma=False,
    )
```

```python
import functools

import jax
import jax.numpy as jnp
from jax import lax
from jax.experimental import pallas as pl
from jax.experimental.pallas import tpu as pltpu
from jax.sharding import PartitionSpec as P

MESH = pl.DeviceIdType.MESH


def kernel(
    workers,
    parts,
    slots,
    chunks,
    moved,
    b_alpha_hbm,
    b_beta_hbm,
    vir_alpha_hbm,
    vir_beta_hbm,
    occ_alpha_hbm,
    occ_beta_hbm,
    row_orbital_hbm,
    pair_list_hbm,
    live_mask_hbm,
    gamma_alpha,
    gamma_beta,
    b_alpha,
    b_beta,
    eps_vir_alpha,
    eps_vir_beta,
    eps_occ_alpha,
    eps_occ_beta,
    row_orbital,
    pair_list,
    live_mask,
    send_block,
    block_j,
    half_send,
    half_recv,
    cross_send,
    cross_recv,
    amp,
    term_send,
    term_recv,
    sum_send,
    sum_recv,
    in_sems,
    fetch_sems,
    half_sems,
    cross_sems,
    pair_sems,
    term_sems,
    alpha_sems,
    sum_sems,
):
    rows, nvir, cols = b_alpha.shape
    chips = parts // 2
    half = nvir // 2
    width = nvir // chunks
    worker = lax.axis_index("occ")
    me = lax.axis_index("aux")
    chip, core = me // 2, lax.rem(me, 2)
    partner = me + 1 - 2 * core
    odd = lax.rem(worker, 2)
    turn = 1 - 2 * odd if moved else 0
    stride = workers // slots
    distances = [k * stride + (0 if moved else 1) for k in range(slots)]
    ahead = [lax.rem(worker + d, workers) for d in distances]
    behind = [lax.rem(worker + workers - d, workers) for d in distances]
    slot = [lax.rem(k + slots - odd, slots) if moved else k for k in range(slots)]
    owner = worker + turn
    others = [lax.rem(chip + k, chips) for k in range(1, chips)]

    each = range(slots)
    local = 1 if moved else 0
    away = range(local, slots)
    hops = range(chips - 1)
    steps = range(chunks)
    spans = [pl.ds(c * width, width) for c in steps]

    loads = [
        pltpu.make_async_copy(src, dst, in_sems.at[n])
        for n, (src, dst) in enumerate(
            [
                (b_beta_hbm, b_beta),
                (row_orbital_hbm, row_orbital),
                (pair_list_hbm, pair_list),
                (live_mask_hbm, live_mask),
                (occ_alpha_hbm, eps_occ_alpha),
                (occ_beta_hbm, eps_occ_beta),
                (vir_alpha_hbm, eps_vir_alpha),
                (vir_beta_hbm, eps_vir_beta),
            ]
            + ([] if moved else [(b_alpha_hbm, b_alpha)])
        )
    ]
    for load in loads:
        load.start()
    barrier = pltpu.get_barrier_semaphore()
    greeted = [ahead[k] for k in away] + [behind[k] for k in away] + ([owner] if moved else [])
    for target in greeted:
        pl.semaphore_signal(barrier, inc=1, device_id={"occ": target}, device_id_type=MESH)
    for peer in [partner] + [other * 2 + core for other in others]:
        pl.semaphore_signal(barrier, inc=1, device_id={"aux": peer}, device_id_type=MESH)
    for load in loads[:3]:
        load.wait()

    def local_row(holder, label):
        found = jnp.int32(0)
        for r in range(rows):
            found = jnp.where(row_orbital[holder * rows + r] == label, r, found)
        return found

    row_i = [local_row(owner, pair_list[slot[k], 0, owner]) for k in each]
    row_out = [local_row(worker, pair_list[slot[k], 1, ahead[k] + turn]) for k in each]

    def remote(src, dst, sems, index, where):
        return pltpu.make_async_remote_copy(
            src_ref=src,
            dst_ref=dst,
            send_sem=sems.at[(0,) + index],
            recv_sem=sems.at[(1,) + index],
            device_id=where,
            device_id_type=MESH,
        )

    alphas = [
        remote(b_alpha_hbm.at[r], b_alpha.at[r], alpha_sems, (r,), {"occ": owner})
        for r in range(rows if moved else 0)
    ]
    fetches = [
        {
            k: remote(
                send_block.at[k - local, spans[c]], block_j.at[k, spans[c]], fetch_sems,
                (c, k - local), {"occ": ahead[k]},
            )
            for k in away
        }
        for c in steps
    ]
    halves = [
        remote(half_send.at[c, 1 - core], half_recv.at[c], half_sems, (c,), {"aux": partner})
        for c in steps
    ]
    crosses = [
        [
            remote(
                cross_send.at[c], cross_recv.at[c, k], cross_sems, (c, k),
                {"aux": others[k] * 2 + core},
            )
            for k in hops
        ]
        for c in steps
    ]
    nears = [
        remote(amp.at[c, core], amp.at[c, core], pair_sems, (c,), {"aux": partner}) for c in steps
    ]
    returns = [
        {
            k: remote(
                term_send.at[k - local, spans[c]], term_recv.at[k - local, spans[c]], term_sems,
                (c, k - local), {"occ": behind[k]},
            )
            for k in away
        }
        for c in steps
    ]
    band = nvir // parts
    bands = [pl.ds(n * band, band) for n in range(parts)]
    sends = [
        remote(sum_send.at[:, bands[n]], sum_recv.at[:, bands[n]], sum_sems, (n,), {"occ": owner})
        for n in range(parts if moved else 0)
    ]

    for k in away:
        send_block[k - local, spans[0]] = b_beta[row_out[k], spans[0]]
    pl.semaphore_wait(barrier, len(greeted) + chips)
    for k in away:
        fetches[0][k].start()
    for copy in alphas:
        copy.start()
    for c in steps[1:]:
        for k in away:
            send_block[k - local, spans[c]] = b_beta[row_out[k], spans[c]]
            fetches[c][k].start()
    for k in range(local):
        block_j[k] = b_beta[row_out[k]]
    for load in loads[3:]:
        load.wait()

    vir_row = eps_vir_alpha[pl.ds(core, 1), :]
    vir_column = jnp.broadcast_to(vir_row, (128, half)).T[:, :1]
    for copy in alphas:
        copy.wait_recv()

    def sums(c):
        for k in each:
            if k in away:
                fetches[c][k].wait_recv()
            partial = lax.dot_general(
                b_alpha[row_i[k]],
                block_j[k, spans[c]],
                (((1,), (1,)), ((), ())),
                preferred_element_type=jnp.float32,
            )
            half_send[c, :, k] = partial.astype(jnp.bfloat16).reshape(2, half, width)
        halves[c].start()

    def pair_sum(c, k):
        return half_send[c, core, k].astype(jnp.float32) + half_recv[c, k].astype(jnp.float32)

    def crossing(c):
        halves[c].wait_recv()
        for k in each:
            cross_send[c, k] = pair_sum(c, k).astype(jnp.bfloat16)
        for copy in crosses[c]:
            copy.start()

    def amplitude(c):
        for copy in crosses[c]:
            copy.wait_recv()
        gap = vir_column + eps_vir_beta[:, spans[c]]
        for k in each:
            total = pair_sum(c, k)
            for n in hops:
                total = total + cross_recv[c, n, k].astype(jnp.float32)
            occ_alpha = eps_occ_alpha[pair_list[slot[k], 0, owner]]
            occ_beta = eps_occ_beta[pair_list[slot[k], 1, owner]]
            live = live_mask[slot[k], owner].astype(jnp.float32)
            value = live * total / (gap - occ_alpha - occ_beta)
            amp[c, core, k] = value.astype(jnp.bfloat16)
        nears[c].start()

    def terms(c):
        for k in list(away) + list(range(local)):
            term = lax.dot_general(
                amp[c, :, k].reshape(nvir, width),
                b_alpha[row_i[k]],
                (((0,), (0,)), ((), ())),
                preferred_element_type=jnp.float32,
            )
            if k in away:
                term_send[k - local, spans[c]] = term.astype(jnp.bfloat16)
                returns[c][k].start()
            else:
                for r in range(rows):
                    gamma_beta[r, spans[c]] = jnp.where(row_out[k] == r, term, 0.0)

    for c in steps:
        sums(c)
        if c >= 2:
            nears[c - 2].wait_recv()
            terms(c - 2)
        crossing(c)
        if c >= 1:
            amplitude(c - 1)
    for c in steps[-2:-1]:
        nears[c].wait_recv()
        terms(c)
    amplitude(chunks - 1)
    nears[chunks - 1].wait_recv()
    for n in range(parts):
        totals = [jnp.zeros((band, cols), jnp.float32)] * rows
        side, first = divmod(n * band, half)
        for k in each:
            left = jnp.concatenate([amp[c, side, k, pl.ds(first, band)] for c in steps], axis=1)
            term = jnp.dot(left, block_j[k], preferred_element_type=jnp.float32)
            totals = [totals[r] + jnp.where(row_i[k] == r, term, 0.0) for r in range(rows)]
        for r in range(rows):
            if moved:
                sum_send[r, bands[n]] = totals[r].astype(jnp.bfloat16)
            else:
                gamma_alpha[r, bands[n]] = totals[r]
        if moved:
            sends[n].start()
    terms(chunks - 1)
    for n, copy in enumerate(sends):
        copy.wait_recv()
        gamma_alpha[:, bands[n]] = sum_recv[:, bands[n]].astype(jnp.float32)
    for c in steps:
        for k in away:
            returns[c][k].wait_recv()
        for r in range(rows):
            total = gamma_beta[r, spans[c]] if local else jnp.zeros((width, cols), jnp.float32)
            for k in away:
                total = total + jnp.where(
                    row_out[k] == r, term_recv[k - local, spans[c]].astype(jnp.float32), 0.0
                )
            gamma_beta[r, spans[c]] = total
    for copy in alphas + sends:
        copy.wait_send()
    for c in steps:
        for copy in [fetches[c][k] for k in away] + [returns[c][k] for k in away]:
            copy.wait_send()
        for copy in [halves[c], nears[c]] + crosses[c]:
            copy.wait_send()


def solution(mesh):
    workers, parts = mesh.shape["occ"], mesh.shape["aux"]

    def shards(
        b_alpha,
        b_beta,
        eps_occ_alpha,
        eps_occ_beta,
        eps_vir_alpha,
        eps_vir_beta,
        row_orbital,
        pair_list,
        live_mask,
    ):
        rows, nvir, cols = b_alpha.shape
        slots = pair_list.shape[0]
        half = nvir // 2
        chips = parts // 2
        vmem = pl.BlockSpec(memory_space=pltpu.VMEM)
        hbm = pl.BlockSpec(memory_space=pltpu.HBM)
        gamma = jax.ShapeDtypeStruct((rows, nvir, cols), jnp.float32)
        moved = workers == 2 * slots
        remote_slots = slots - 1 if moved else slots
        block = pltpu.VMEM((slots, nvir, cols), jnp.bfloat16)
        sent = pltpu.VMEM((remote_slots, nvir, cols), jnp.bfloat16)
        totals = pltpu.VMEM(b_alpha.shape, jnp.bfloat16)
        chunks = max(1, nvir // 128)
        piece = (slots, half, nvir // chunks)
        block_copies = pltpu.SemaphoreType.DMA((2, chunks, remote_slots))
        copies = pltpu.SemaphoreType.DMA((2, chunks))
        hop_copies = pltpu.SemaphoreType.DMA((2, chunks, chips - 1))
        pairs = jnp.transpose(pair_list, (0, 2, 1))
        return pl.pallas_call(
            functools.partial(kernel, workers, parts, slots, chunks, moved),
            out_shape=(gamma, gamma),
            in_specs=[hbm] * 9,
            out_specs=(vmem, vmem),
            scratch_shapes=[
                pltpu.VMEM(b_alpha.shape, b_alpha.dtype),
                pltpu.VMEM(b_beta.shape, b_beta.dtype),
                pltpu.VMEM((2, half), jnp.float32),
                pltpu.VMEM((1, nvir), jnp.float32),
                pltpu.SMEM(eps_occ_alpha.shape, jnp.float32),
                pltpu.SMEM(eps_occ_beta.shape, jnp.float32),
                pltpu.SMEM(row_orbital.shape, jnp.int32),
                pltpu.SMEM(pairs.shape, jnp.int32),
                pltpu.SMEM(live_mask.shape, jnp.int32),
                sent,
                block,
                pltpu.VMEM((chunks, 2) + piece, jnp.bfloat16),
                pltpu.VMEM((chunks,) + piece, jnp.bfloat16),
                pltpu.VMEM((chunks,) + piece, jnp.bfloat16),
                pltpu.VMEM((chunks, chips - 1) + piece, jnp.bfloat16),
                pltpu.VMEM((chunks, 2) + piece, jnp.bfloat16),
                sent,
                sent,
                totals,
                totals,
                pltpu.SemaphoreType.DMA((9,)),
                block_copies,
                copies,
                hop_copies,
                copies,
                block_copies,
                pltpu.SemaphoreType.DMA((2, rows)),
                pltpu.SemaphoreType.DMA((2, parts)),
            ],
            compiler_params=pltpu.CompilerParams(
                collective_id=0, has_side_effects=True, vmem_limit_bytes=56 * 1024 * 1024
            ),
        )(
            b_alpha,
            b_beta,
            eps_vir_alpha.reshape(2, half),
            eps_vir_beta.reshape(1, nvir),
            eps_occ_alpha,
            eps_occ_beta,
            row_orbital,
            pairs,
            live_mask,
        )

    placed = (P("occ", None, "aux"), P("occ", None, "aux"), P(), P(), P(), P(), P(), P(), P())
    return jax.shard_map(
        shards,
        mesh=mesh,
        in_specs=placed,
        out_specs=(P("occ", None, "aux"), P("occ", None, "aux")),
        check_vma=False,
    )
```

```python
import functools

import jax
import jax.numpy as jnp
from jax import lax
from jax.experimental import pallas as pl
from jax.experimental.pallas import tpu as pltpu
from jax.sharding import PartitionSpec as P

MESH = pl.DeviceIdType.MESH


def kernel(
    workers,
    parts,
    slots,
    chunks,
    moved,
    b_alpha_hbm,
    b_beta_hbm,
    vir_alpha_hbm,
    vir_beta_hbm,
    occ_alpha_hbm,
    occ_beta_hbm,
    row_orbital_hbm,
    pair_list_hbm,
    live_mask_hbm,
    gamma_alpha,
    gamma_beta,
    b_alpha,
    b_beta,
    eps_vir_alpha,
    eps_vir_beta,
    eps_occ_alpha,
    eps_occ_beta,
    row_orbital,
    pair_list,
    live_mask,
    send_block,
    block_j,
    half_send,
    half_recv,
    cross_send,
    cross_recv,
    amp,
    term_send,
    term_recv,
    sum_send,
    sum_recv,
    in_sems,
    fetch_sems,
    half_sems,
    cross_sems,
    pair_sems,
    term_sems,
    alpha_sems,
    sum_sems,
):
    rows, nvir, cols = b_alpha.shape
    chips = parts // 2
    half = nvir // 2
    width = nvir // chunks
    worker = lax.axis_index("occ")
    me = lax.axis_index("aux")
    chip, core = me // 2, lax.rem(me, 2)
    partner = me + 1 - 2 * core
    odd = lax.rem(worker, 2)
    turn = 1 - 2 * odd if moved else 0
    stride = workers // slots
    distances = [k * stride + (0 if moved else 1) for k in range(slots)]
    ahead = [lax.rem(worker + d, workers) for d in distances]
    behind = [lax.rem(worker + workers - d, workers) for d in distances]
    slot = [lax.rem(k + slots - odd, slots) if moved else k for k in range(slots)]
    owner = worker + turn
    others = [lax.rem(chip + k, chips) for k in range(1, chips)]

    each = range(slots)
    local = 1 if moved else 0
    away = range(local, slots)
    hops = range(chips - 1)
    steps = range(chunks)
    spans = [pl.ds(c * width, width) for c in steps]

    loads = [
        pltpu.make_async_copy(src, dst, in_sems.at[n])
        for n, (src, dst) in enumerate(
            [
                (b_beta_hbm, b_beta),
                (row_orbital_hbm, row_orbital),
                (pair_list_hbm, pair_list),
                (live_mask_hbm, live_mask),
                (occ_alpha_hbm, eps_occ_alpha),
                (occ_beta_hbm, eps_occ_beta),
                (vir_alpha_hbm, eps_vir_alpha),
                (vir_beta_hbm, eps_vir_beta),
            ]
            + ([] if moved else [(b_alpha_hbm, b_alpha)])
        )
    ]
    for load in loads:
        load.start()
    barrier = pltpu.get_barrier_semaphore()
    greeted = [ahead[k] for k in away] + [behind[k] for k in away] + ([owner] if moved else [])
    for target in greeted:
        pl.semaphore_signal(barrier, inc=1, device_id={"occ": target}, device_id_type=MESH)
    for peer in [partner] + [other * 2 + core for other in others]:
        pl.semaphore_signal(barrier, inc=1, device_id={"aux": peer}, device_id_type=MESH)
    for load in loads[:3]:
        load.wait()

    def local_row(holder, label):
        found = jnp.int32(0)
        for r in range(rows):
            found = jnp.where(row_orbital[holder * rows + r] == label, r, found)
        return found

    row_i = [local_row(owner, pair_list[slot[k], 0, owner]) for k in each]
    row_out = [local_row(worker, pair_list[slot[k], 1, ahead[k] + turn]) for k in each]

    def remote(src, dst, sems, index, where):
        return pltpu.make_async_remote_copy(
            src_ref=src,
            dst_ref=dst,
            send_sem=sems.at[(0,) + index],
            recv_sem=sems.at[(1,) + index],
            device_id=where,
            device_id_type=MESH,
        )

    alphas = [
        remote(b_alpha_hbm.at[r], b_alpha.at[r], alpha_sems, (r,), {"occ": owner})
        for r in range(rows if moved else 0)
    ]
    fetches = [
        {
            k: remote(
                send_block.at[k - local, spans[c]], block_j.at[k, spans[c]], fetch_sems,
                (c, k - local), {"occ": ahead[k]},
            )
            for k in away
        }
        for c in steps
    ]
    halves = [
        remote(half_send.at[c, 1 - core], half_recv.at[c], half_sems, (c,), {"aux": partner})
        for c in steps
    ]
    crosses = [
        [
            remote(
                cross_send.at[c], cross_recv.at[c, k], cross_sems, (c, k),
                {"aux": others[k] * 2 + core},
            )
            for k in hops
        ]
        for c in steps
    ]
    nears = [
        remote(amp.at[c, core], amp.at[c, core], pair_sems, (c,), {"aux": partner}) for c in steps
    ]
    returns = [
        {
            k: remote(
                term_send.at[k - local, spans[c]], term_recv.at[k - local, spans[c]], term_sems,
                (c, k - local), {"occ": behind[k]},
            )
            for k in away
        }
        for c in steps
    ]
    band = nvir // parts
    bands = [pl.ds(n * band, band) for n in range(parts)]
    sends = [
        remote(sum_send.at[:, bands[n]], sum_recv.at[:, bands[n]], sum_sems, (n,), {"occ": owner})
        for n in range(parts if moved else 0)
    ]

    for k in away:
        send_block[k - local, spans[0]] = b_beta[row_out[k], spans[0]]
    pl.semaphore_wait(barrier, len(greeted) + chips)
    for k in away:
        fetches[0][k].start()
    for copy in alphas:
        copy.start()
    for c in steps[1:]:
        for k in away:
            send_block[k - local, spans[c]] = b_beta[row_out[k], spans[c]]
            fetches[c][k].start()
    for k in range(local):
        block_j[k] = b_beta[row_out[k]]
    for load in loads[3:]:
        load.wait()

    vir_row = eps_vir_alpha[:, pl.ds(pl.multiple_of(core * half, half), half)]
    vir_column = jnp.broadcast_to(vir_row, (128, half)).T[:, :1]
    for copy in alphas:
        copy.wait_recv()

    def sums(c):
        for k in each:
            if k in away:
                fetches[c][k].wait_recv()
            partial = lax.dot_general(
                b_alpha[row_i[k]],
                block_j[k, spans[c]],
                (((1,), (1,)), ((), ())),
                preferred_element_type=jnp.float32,
            )
            half_send[c, :, k] = partial.astype(jnp.bfloat16).reshape(2, half, width)
        halves[c].start()

    def pair_sum(c, k):
        return half_send[c, core, k].astype(jnp.float32) + half_recv[c, k].astype(jnp.float32)

    def crossing(c):
        halves[c].wait_recv()
        for k in each:
            cross_send[c, k] = pair_sum(c, k).astype(jnp.bfloat16)
        for copy in crosses[c]:
            copy.start()

    def amplitude(c):
        for copy in crosses[c]:
            copy.wait_recv()
        gap = vir_column + eps_vir_beta[:, spans[c]]
        for k in each:
            total = pair_sum(c, k)
            for n in hops:
                total = total + cross_recv[c, n, k].astype(jnp.float32)
            occ_alpha = eps_occ_alpha[pair_list[slot[k], 0, owner]]
            occ_beta = eps_occ_beta[pair_list[slot[k], 1, owner]]
            live = live_mask[slot[k], owner].astype(jnp.float32)
            value = live * total / (gap - occ_alpha - occ_beta)
            amp[c, core, k] = value.astype(jnp.bfloat16)
        nears[c].start()

    def terms(c):
        for k in list(away) + list(range(local)):
            term = lax.dot_general(
                amp[c, :, k].reshape(nvir, width),
                b_alpha[row_i[k]],
                (((0,), (0,)), ((), ())),
                preferred_element_type=jnp.float32,
            )
            if k in away:
                term_send[k - local, spans[c]] = term.astype(jnp.bfloat16)
                returns[c][k].start()
            else:
                for r in range(rows):
                    gamma_beta[r, spans[c]] = jnp.where(row_out[k] == r, term, 0.0)

    def finished(c):
        nears[c].wait_recv()
        terms(c)

    for c in steps:
        sums(c)
        if c >= 1 and c == chunks - 1:
            for n in steps[: c - 1]:
                finished(n)
        crossing(c)
        if c >= 1:
            amplitude(c - 1)
    for c in steps[-2:-1]:
        finished(c)
    amplitude(chunks - 1)
    nears[chunks - 1].wait_recv()
    for n in range(parts):
        totals = [jnp.zeros((band, cols), jnp.float32)] * rows
        side, first = divmod(n * band, half)
        for k in each:
            left = jnp.concatenate([amp[c, side, k, pl.ds(first, band)] for c in steps], axis=1)
            term = jnp.dot(left, block_j[k], preferred_element_type=jnp.float32)
            totals = [totals[r] + jnp.where(row_i[k] == r, term, 0.0) for r in range(rows)]
        for r in range(rows):
            if moved:
                sum_send[r, bands[n]] = totals[r].astype(jnp.bfloat16)
            else:
                gamma_alpha[r, bands[n]] = totals[r]
        if moved:
            sends[n].start()
    terms(chunks - 1)
    for n, copy in enumerate(sends):
        copy.wait_recv()
        gamma_alpha[:, bands[n]] = sum_recv[:, bands[n]].astype(jnp.float32)
    for c in steps:
        for k in away:
            returns[c][k].wait_recv()
        for r in range(rows):
            total = gamma_beta[r, spans[c]] if local else jnp.zeros((width, cols), jnp.float32)
            for k in away:
                total = total + jnp.where(
                    row_out[k] == r, term_recv[k - local, spans[c]].astype(jnp.float32), 0.0
                )
            gamma_beta[r, spans[c]] = total
    for copy in alphas + sends:
        copy.wait_send()
    for c in steps:
        for copy in [fetches[c][k] for k in away] + [returns[c][k] for k in away]:
            copy.wait_send()
        for copy in [halves[c], nears[c]] + crosses[c]:
            copy.wait_send()


def solution(mesh):
    workers, parts = mesh.shape["occ"], mesh.shape["aux"]

    def shards(
        b_alpha,
        b_beta,
        eps_occ_alpha,
        eps_occ_beta,
        eps_vir_alpha,
        eps_vir_beta,
        row_orbital,
        pair_list,
        live_mask,
    ):
        rows, nvir, cols = b_alpha.shape
        slots = pair_list.shape[0]
        half = nvir // 2
        chips = parts // 2
        vmem = pl.BlockSpec(memory_space=pltpu.VMEM)
        hbm = pl.BlockSpec(memory_space=pltpu.HBM)
        gamma = jax.ShapeDtypeStruct((rows, nvir, cols), jnp.float32)
        moved = workers == 2 * slots
        remote_slots = slots - 1 if moved else slots
        block = pltpu.VMEM((slots, nvir, cols), jnp.bfloat16)
        sent = pltpu.VMEM((remote_slots, nvir, cols), jnp.bfloat16)
        totals = pltpu.VMEM(b_alpha.shape, jnp.bfloat16)
        chunks = max(1, nvir // 128)
        piece = (slots, half, nvir // chunks)
        block_copies = pltpu.SemaphoreType.DMA((2, chunks, remote_slots))
        copies = pltpu.SemaphoreType.DMA((2, chunks))
        hop_copies = pltpu.SemaphoreType.DMA((2, chunks, chips - 1))
        pairs = jnp.transpose(pair_list, (0, 2, 1))
        return pl.pallas_call(
            functools.partial(kernel, workers, parts, slots, chunks, moved),
            out_shape=(gamma, gamma),
            in_specs=[hbm] * 9,
            out_specs=(vmem, vmem),
            scratch_shapes=[
                pltpu.VMEM(b_alpha.shape, b_alpha.dtype),
                pltpu.VMEM(b_beta.shape, b_beta.dtype),
                pltpu.VMEM((1, nvir), jnp.float32),
                pltpu.VMEM((1, nvir), jnp.float32),
                pltpu.SMEM(eps_occ_alpha.shape, jnp.float32),
                pltpu.SMEM(eps_occ_beta.shape, jnp.float32),
                pltpu.SMEM(row_orbital.shape, jnp.int32),
                pltpu.SMEM(pairs.shape, jnp.int32),
                pltpu.SMEM(live_mask.shape, jnp.int32),
                sent,
                block,
                pltpu.VMEM((chunks, 2) + piece, jnp.bfloat16),
                pltpu.VMEM((chunks,) + piece, jnp.bfloat16),
                pltpu.VMEM((chunks,) + piece, jnp.bfloat16),
                pltpu.VMEM((chunks, chips - 1) + piece, jnp.bfloat16),
                pltpu.VMEM((chunks, 2) + piece, jnp.bfloat16),
                sent,
                sent,
                totals,
                totals,
                pltpu.SemaphoreType.DMA((9,)),
                block_copies,
                copies,
                hop_copies,
                copies,
                block_copies,
                pltpu.SemaphoreType.DMA((2, rows)),
                pltpu.SemaphoreType.DMA((2, parts)),
            ],
            compiler_params=pltpu.CompilerParams(
                collective_id=0, has_side_effects=True, vmem_limit_bytes=56 * 1024 * 1024
            ),
        )(
            b_alpha,
            b_beta,
            eps_vir_alpha.reshape(1, nvir),
            eps_vir_beta.reshape(1, nvir),
            eps_occ_alpha,
            eps_occ_beta,
            row_orbital,
            pairs,
            live_mask,
        )

    placed = (P("occ", None, "aux"), P("occ", None, "aux"), P(), P(), P(), P(), P(), P(), P())
    return jax.shard_map(
        shards,
        mesh=mesh,
        in_specs=placed,
        out_specs=(P("occ", None, "aux"), P("occ", None, "aux")),
        check_vma=False,
    )
```

```python
import functools

import jax
import jax.numpy as jnp
from jax import lax
from jax.experimental import pallas as pl
from jax.experimental.pallas import tpu as pltpu
from jax.sharding import PartitionSpec as P

MESH = pl.DeviceIdType.MESH


def kernel(
    workers,
    parts,
    slots,
    chunks,
    moved,
    b_alpha_hbm,
    b_beta_hbm,
    vir_alpha_hbm,
    vir_beta_hbm,
    occ_alpha_hbm,
    occ_beta_hbm,
    row_orbital_hbm,
    pair_list_hbm,
    live_mask_hbm,
    alpha_sums,
    gamma_beta,
    b_alpha,
    b_beta,
    eps_vir_alpha,
    eps_vir_beta,
    eps_occ_alpha,
    eps_occ_beta,
    row_orbital,
    pair_list,
    live_mask,
    send_block,
    block_j,
    half_send,
    half_recv,
    cross_send,
    cross_recv,
    amp,
    term_send,
    term_recv,
    sum_send,
    in_sems,
    fetch_sems,
    half_sems,
    cross_sems,
    pair_sems,
    term_sems,
    alpha_sems,
    sum_sems,
):
    rows, nvir, cols = b_alpha.shape
    chips = parts // 2
    half = nvir // 2
    width = nvir // chunks
    worker = lax.axis_index("occ")
    me = lax.axis_index("aux")
    chip, core = me // 2, lax.rem(me, 2)
    partner = me + 1 - 2 * core
    odd = lax.rem(worker, 2)
    turn = 1 - 2 * odd if moved else 0
    stride = workers // slots
    distances = [k * stride + (0 if moved else 1) for k in range(slots)]
    ahead = [lax.rem(worker + d, workers) for d in distances]
    behind = [lax.rem(worker + workers - d, workers) for d in distances]
    slot = [lax.rem(k + slots - odd, slots) if moved else k for k in range(slots)]
    owner = worker + turn
    others = [lax.rem(chip + k, chips) for k in range(1, chips)]

    each = range(slots)
    local = 1 if moved else 0
    away = range(local, slots)
    hops = range(chips - 1)
    steps = range(chunks)
    spans = [pl.ds(c * width, width) for c in steps]

    loads = [
        pltpu.make_async_copy(src, dst, in_sems.at[n])
        for n, (src, dst) in enumerate(
            [
                (b_beta_hbm, b_beta),
                (row_orbital_hbm, row_orbital),
                (pair_list_hbm, pair_list),
                (live_mask_hbm, live_mask),
                (occ_alpha_hbm, eps_occ_alpha),
                (occ_beta_hbm, eps_occ_beta),
                (vir_alpha_hbm, eps_vir_alpha),
                (vir_beta_hbm, eps_vir_beta),
            ]
            + ([] if moved else [(b_alpha_hbm, b_alpha)])
        )
    ]
    for load in loads:
        load.start()
    barrier = pltpu.get_barrier_semaphore()
    greeted = [ahead[k] for k in away] + [behind[k] for k in away] + ([owner] if moved else [])
    for target in greeted:
        pl.semaphore_signal(barrier, inc=1, device_id={"occ": target}, device_id_type=MESH)
    for peer in [partner] + [other * 2 + core for other in others]:
        pl.semaphore_signal(barrier, inc=1, device_id={"aux": peer}, device_id_type=MESH)
    for load in loads[:3]:
        load.wait()

    def local_row(holder, label):
        found = jnp.int32(0)
        for r in range(rows):
            found = jnp.where(row_orbital[holder * rows + r] == label, r, found)
        return found

    row_i = [local_row(owner, pair_list[slot[k], 0, owner]) for k in each]
    row_out = [local_row(worker, pair_list[slot[k], 1, ahead[k] + turn]) for k in each]

    def remote(src, dst, sems, index, where):
        return pltpu.make_async_remote_copy(
            src_ref=src,
            dst_ref=dst,
            send_sem=sems.at[(0,) + index],
            recv_sem=sems.at[(1,) + index],
            device_id=where,
            device_id_type=MESH,
        )

    alphas = [
        remote(b_alpha_hbm.at[r], b_alpha.at[r], alpha_sems, (r,), {"occ": owner})
        for r in range(rows if moved else 0)
    ]
    fetches = [
        {
            k: remote(
                send_block.at[k - local, spans[c]], block_j.at[k, spans[c]], fetch_sems,
                (c, k - local), {"occ": ahead[k]},
            )
            for k in away
        }
        for c in steps
    ]
    halves = [
        remote(half_send.at[c, 1 - core], half_recv.at[c], half_sems, (c,), {"aux": partner})
        for c in steps
    ]
    crosses = [
        [
            remote(
                cross_send.at[c], cross_recv.at[c, k], cross_sems, (c, k),
                {"aux": others[k] * 2 + core},
            )
            for k in hops
        ]
        for c in steps
    ]
    nears = [
        remote(amp.at[c, core], amp.at[c, core], pair_sems, (c,), {"aux": partner}) for c in steps
    ]
    returns = [
        {
            k: remote(
                term_send.at[k - local, spans[c]], term_recv.at[k - local, spans[c]], term_sems,
                (c, k - local), {"occ": behind[k]},
            )
            for k in away
        }
        for c in steps
    ]
    band = nvir // parts
    bands = [pl.ds(n * band, band) for n in range(parts)]
    sends = [
        remote(sum_send.at[:, bands[n]], alpha_sums.at[:, bands[n]], sum_sems, (n,), {"occ": owner})
        for n in range(parts if moved else 0)
    ]

    for k in away:
        send_block[k - local, spans[0]] = b_beta[row_out[k], spans[0]]
    pl.semaphore_wait(barrier, len(greeted) + chips)
    for k in away:
        fetches[0][k].start()
    for copy in alphas:
        copy.start()
    for c in steps[1:]:
        for k in away:
            send_block[k - local, spans[c]] = b_beta[row_out[k], spans[c]]
            fetches[c][k].start()
    for k in range(local):
        block_j[k] = b_beta[row_out[k]]
    for load in loads[3:]:
        load.wait()

    vir_row = eps_vir_alpha[:, pl.ds(pl.multiple_of(core * half, half), half)]
    vir_column = jnp.broadcast_to(vir_row, (128, half)).T[:, :1]
    for copy in alphas:
        copy.wait_recv()

    def sums(c):
        for k in each:
            if k in away:
                fetches[c][k].wait_recv()
            partial = lax.dot_general(
                b_alpha[row_i[k]],
                block_j[k, spans[c]],
                (((1,), (1,)), ((), ())),
                preferred_element_type=jnp.float32,
            )
            half_send[c, :, k] = partial.astype(jnp.bfloat16).reshape(2, half, width)
        halves[c].start()

    def pair_sum(c, k):
        return half_send[c, core, k].astype(jnp.float32) + half_recv[c, k].astype(jnp.float32)

    def crossing(c):
        halves[c].wait_recv()
        for k in each:
            cross_send[c, k] = pair_sum(c, k).astype(jnp.bfloat16)
        for copy in crosses[c]:
            copy.start()

    def amplitude(c):
        for copy in crosses[c]:
            copy.wait_recv()
        gap = vir_column + eps_vir_beta[:, spans[c]]
        for k in each:
            total = pair_sum(c, k)
            for n in hops:
                total = total + cross_recv[c, n, k].astype(jnp.float32)
            occ_alpha = eps_occ_alpha[pair_list[slot[k], 0, owner]]
            occ_beta = eps_occ_beta[pair_list[slot[k], 1, owner]]
            live = live_mask[slot[k], owner].astype(jnp.float32)
            value = live * total / (gap - occ_alpha - occ_beta)
            amp[c, core, k] = value.astype(jnp.bfloat16)
        nears[c].start()

    def terms(c):
        for k in list(away) + list(range(local)):
            term = lax.dot_general(
                amp[c, :, k].reshape(nvir, width),
                b_alpha[row_i[k]],
                (((0,), (0,)), ((), ())),
                preferred_element_type=jnp.float32,
            )
            if k in away:
                term_send[k - local, spans[c]] = term.astype(jnp.bfloat16)
                returns[c][k].start()
            else:
                for r in range(rows):
                    gamma_beta[r, spans[c]] = jnp.where(row_out[k] == r, term, 0.0)

    def finished(c):
        nears[c].wait_recv()
        terms(c)

    for c in steps:
        sums(c)
        if c >= 1 and c == chunks - 1:
            for n in steps[: c - 1]:
                finished(n)
        crossing(c)
        if c >= 1:
            amplitude(c - 1)
    for c in steps[-2:-1]:
        finished(c)
    amplitude(chunks - 1)
    nears[chunks - 1].wait_recv()
    for n in range(parts):
        totals = [jnp.zeros((band, cols), jnp.float32)] * rows
        side, first = divmod(n * band, half)
        for k in each:
            left = jnp.concatenate([amp[c, side, k, pl.ds(first, band)] for c in steps], axis=1)
            term = jnp.dot(left, block_j[k], preferred_element_type=jnp.float32)
            totals = [totals[r] + jnp.where(row_i[k] == r, term, 0.0) for r in range(rows)]
        for r in range(rows):
            if moved:
                sum_send[r, bands[n]] = totals[r].astype(jnp.bfloat16)
            else:
                alpha_sums[r, bands[n]] = totals[r]
        if moved:
            sends[n].start()
    terms(chunks - 1)
    for c in steps:
        for k in away:
            returns[c][k].wait_recv()
        for r in range(rows):
            total = gamma_beta[r, spans[c]] if local else jnp.zeros((width, cols), jnp.float32)
            for k in away:
                total = total + jnp.where(
                    row_out[k] == r, term_recv[k - local, spans[c]].astype(jnp.float32), 0.0
                )
            gamma_beta[r, spans[c]] = total
    for copy in sends:
        copy.wait_recv()
    for copy in alphas + sends:
        copy.wait_send()
    for c in steps:
        for copy in [fetches[c][k] for k in away] + [returns[c][k] for k in away]:
            copy.wait_send()
        for copy in [halves[c], nears[c]] + crosses[c]:
            copy.wait_send()


def write_out(alpha_sums, beta_sums, gamma_alpha, gamma_beta, wide, sems):
    beta = pltpu.make_async_copy(beta_sums, gamma_beta, sems.at[0])
    beta.start()
    copies = [beta]
    for r in range(wide.shape[0]):
        wide[r] = alpha_sums[r].astype(jnp.float32)
        copies.append(pltpu.make_async_copy(wide.at[r], gamma_alpha.at[r], sems.at[1 + r]))
        copies[-1].start()
    for copy in copies:
        copy.wait()


def solution(mesh):
    workers, parts = mesh.shape["occ"], mesh.shape["aux"]

    def shards(
        b_alpha,
        b_beta,
        eps_occ_alpha,
        eps_occ_beta,
        eps_vir_alpha,
        eps_vir_beta,
        row_orbital,
        pair_list,
        live_mask,
    ):
        rows, nvir, cols = b_alpha.shape
        slots = pair_list.shape[0]
        half = nvir // 2
        chips = parts // 2
        vmem = pl.BlockSpec(memory_space=pltpu.VMEM)
        hbm = pl.BlockSpec(memory_space=pltpu.HBM)
        gamma = jax.ShapeDtypeStruct((rows, nvir, cols), jnp.float32)
        moved = workers == 2 * slots
        remote_slots = slots - 1 if moved else slots
        block = pltpu.VMEM((slots, nvir, cols), jnp.bfloat16)
        sent = pltpu.VMEM((remote_slots, nvir, cols), jnp.bfloat16)
        totals = pltpu.VMEM(b_alpha.shape, jnp.bfloat16)
        chunks = max(1, nvir // 128)
        piece = (slots, half, nvir // chunks)
        block_copies = pltpu.SemaphoreType.DMA((2, chunks, remote_slots))
        copies = pltpu.SemaphoreType.DMA((2, chunks))
        hop_copies = pltpu.SemaphoreType.DMA((2, chunks, chips - 1))
        pairs = jnp.transpose(pair_list, (0, 2, 1))
        sums = pl.pallas_call(
            functools.partial(kernel, workers, parts, slots, chunks, moved),
            out_shape=(
                pltpu.VMEM(gamma.shape, jnp.bfloat16 if moved else jnp.float32),
                pltpu.VMEM(gamma.shape, jnp.float32),
            ),
            in_specs=[hbm] * 9,
            out_specs=(vmem, vmem),
            scratch_shapes=[
                pltpu.VMEM(b_alpha.shape, b_alpha.dtype),
                pltpu.VMEM(b_beta.shape, b_beta.dtype),
                pltpu.VMEM((1, nvir), jnp.float32),
                pltpu.VMEM((1, nvir), jnp.float32),
                pltpu.SMEM(eps_occ_alpha.shape, jnp.float32),
                pltpu.SMEM(eps_occ_beta.shape, jnp.float32),
                pltpu.SMEM(row_orbital.shape, jnp.int32),
                pltpu.SMEM(pairs.shape, jnp.int32),
                pltpu.SMEM(live_mask.shape, jnp.int32),
                sent,
                block,
                pltpu.VMEM((chunks, 2) + piece, jnp.bfloat16),
                pltpu.VMEM((chunks,) + piece, jnp.bfloat16),
                pltpu.VMEM((chunks,) + piece, jnp.bfloat16),
                pltpu.VMEM((chunks, chips - 1) + piece, jnp.bfloat16),
                pltpu.VMEM((chunks, 2) + piece, jnp.bfloat16),
                sent,
                sent,
                totals,
                pltpu.SemaphoreType.DMA((9,)),
                block_copies,
                copies,
                hop_copies,
                copies,
                block_copies,
                pltpu.SemaphoreType.DMA((2, rows)),
                pltpu.SemaphoreType.DMA((2, parts)),
            ],
            compiler_params=pltpu.CompilerParams(
                collective_id=0, has_side_effects=True, vmem_limit_bytes=56 * 1024 * 1024
            ),
        )(
            b_alpha,
            b_beta,
            eps_vir_alpha.reshape(1, nvir),
            eps_vir_beta.reshape(1, nvir),
            eps_occ_alpha,
            eps_occ_beta,
            row_orbital,
            pairs,
            live_mask,
        )
        return pl.pallas_call(
            write_out,
            out_shape=(gamma, gamma),
            in_specs=[vmem] * 2,
            out_specs=(hbm, hbm),
            scratch_shapes=[
                pltpu.VMEM(gamma.shape, jnp.float32),
                pltpu.SemaphoreType.DMA((1 + rows,)),
            ],
            compiler_params=pltpu.CompilerParams(vmem_limit_bytes=16 * 1024 * 1024),
        )(*sums)

    placed = (P("occ", None, "aux"), P("occ", None, "aux"), P(), P(), P(), P(), P(), P(), P())
    return jax.shard_map(
        shards,
        mesh=mesh,
        in_specs=placed,
        out_specs=(P("occ", None, "aux"), P("occ", None, "aux")),
        check_vma=False,
    )
```

```python
import functools

import jax
import jax.numpy as jnp
from jax import lax
from jax.experimental import pallas as pl
from jax.experimental.pallas import tpu as pltpu
from jax.sharding import PartitionSpec as P

MESH = pl.DeviceIdType.MESH


def kernel(
    workers,
    parts,
    slots,
    chunks,
    moved,
    b_alpha_hbm,
    b_beta_hbm,
    vir_alpha_hbm,
    vir_beta_hbm,
    occ_alpha_hbm,
    occ_beta_hbm,
    row_orbital_hbm,
    pair_list_hbm,
    live_mask_hbm,
    alpha_sums,
    gamma_beta,
    b_alpha,
    b_beta,
    eps_vir_alpha,
    eps_vir_beta,
    eps_occ_alpha,
    eps_occ_beta,
    row_orbital,
    pair_list,
    live_mask,
    send_block,
    block_j,
    half_send,
    half_recv,
    cross_send,
    cross_recv,
    amp,
    term_send,
    term_recv,
    sum_send,
    in_sems,
    fetch_sems,
    half_sems,
    cross_sems,
    pair_sems,
    term_sems,
    alpha_sems,
    sum_sems,
):
    rows, nvir, cols = b_alpha.shape
    chips = parts // 2
    half = nvir // 2
    width = nvir // chunks
    worker = lax.axis_index("occ")
    me = lax.axis_index("aux")
    chip, core = me // 2, lax.rem(me, 2)
    partner = me + 1 - 2 * core
    odd = lax.rem(worker, 2)
    turn = 1 - 2 * odd if moved else 0
    stride = workers // slots
    distances = [k * stride + (0 if moved else 1) for k in range(slots)]
    ahead = [lax.rem(worker + d, workers) for d in distances]
    behind = [lax.rem(worker + workers - d, workers) for d in distances]
    slot = [lax.rem(k + slots - odd, slots) if moved else k for k in range(slots)]
    owner = worker + turn
    others = [lax.rem(chip + k, chips) for k in range(1, chips)]

    each = range(slots)
    local = 1 if moved else 0
    away = range(local, slots)
    hops = range(chips - 1)
    steps = range(chunks)
    spans = [pl.ds(c * width, width) for c in steps]

    loads = [
        pltpu.make_async_copy(src, dst, in_sems.at[n])
        for n, (src, dst) in enumerate(
            [
                (b_beta_hbm, b_beta),
                (row_orbital_hbm, row_orbital),
                (pair_list_hbm, pair_list),
                (live_mask_hbm, live_mask),
                (occ_alpha_hbm, eps_occ_alpha),
                (occ_beta_hbm, eps_occ_beta),
                (vir_alpha_hbm, eps_vir_alpha),
                (vir_beta_hbm, eps_vir_beta),
            ]
            + ([] if moved else [(b_alpha_hbm, b_alpha)])
        )
    ]
    for load in loads:
        load.start()
    barrier = pltpu.get_barrier_semaphore()
    greeted = [ahead[k] for k in away] + [behind[k] for k in away] + ([owner] if moved else [])
    for target in greeted:
        pl.semaphore_signal(barrier, inc=1, device_id={"occ": target}, device_id_type=MESH)
    for peer in [partner] + [other * 2 + core for other in others]:
        pl.semaphore_signal(barrier, inc=1, device_id={"aux": peer}, device_id_type=MESH)
    for load in loads[:3]:
        load.wait()

    def local_row(holder, label):
        found = jnp.int32(0)
        for r in range(rows):
            found = jnp.where(row_orbital[holder * rows + r] == label, r, found)
        return found

    row_i = [local_row(owner, pair_list[slot[k], 0, owner]) for k in each]
    row_out = [local_row(worker, pair_list[slot[k], 1, ahead[k] + turn]) for k in each]

    def remote(src, dst, sems, index, where):
        return pltpu.make_async_remote_copy(
            src_ref=src,
            dst_ref=dst,
            send_sem=sems.at[(0,) + index],
            recv_sem=sems.at[(1,) + index],
            device_id=where,
            device_id_type=MESH,
        )

    alphas = [
        remote(b_alpha_hbm.at[r], b_alpha.at[r], alpha_sems, (r,), {"occ": owner})
        for r in range(rows if moved else 0)
    ]
    fetches = [
        {
            k: remote(
                send_block.at[k - local, spans[c]], block_j.at[k, spans[c]], fetch_sems,
                (c, k - local), {"occ": ahead[k]},
            )
            for k in away
        }
        for c in steps
    ]
    halves = [
        remote(half_send.at[c, 1 - core], half_recv.at[c], half_sems, (c,), {"aux": partner})
        for c in steps
    ]
    crosses = [
        [
            remote(
                cross_send.at[c], cross_recv.at[c, k], cross_sems, (c, k),
                {"aux": others[k] * 2 + core},
            )
            for k in hops
        ]
        for c in steps
    ]
    nears = [
        remote(amp.at[c, core], amp.at[c, core], pair_sems, (c,), {"aux": partner}) for c in steps
    ]
    returns = [
        {
            k: remote(
                term_send.at[k - local, spans[c]], term_recv.at[k - local, spans[c]], term_sems,
                (c, k - local), {"occ": behind[k]},
            )
            for k in away
        }
        for c in steps
    ]
    band = nvir // parts
    bands = [pl.ds(n * band, band) for n in range(parts)]
    sends = [
        remote(sum_send.at[:, bands[n]], alpha_sums.at[:, bands[n]], sum_sems, (n,), {"occ": owner})
        for n in range(parts if moved else 0)
    ]

    for k in away:
        send_block[k - local, spans[0]] = b_beta[row_out[k], spans[0]]
    pl.semaphore_wait(barrier, len(greeted) + chips)
    for k in away:
        fetches[0][k].start()
    for copy in alphas:
        copy.start()
    for c in steps[1:]:
        for k in away:
            send_block[k - local, spans[c]] = b_beta[row_out[k], spans[c]]
            fetches[c][k].start()
    for k in range(local):
        block_j[k] = b_beta[row_out[k]]
    for load in loads[3:]:
        load.wait()

    vir_row = eps_vir_alpha[:, pl.ds(pl.multiple_of(core * half, half), half)]
    vir_column = jnp.broadcast_to(vir_row, (128, half)).T[:, :1]
    for copy in alphas:
        copy.wait_recv()

    def sums(c):
        for k in each:
            if k in away:
                fetches[c][k].wait_recv()
            partial = lax.dot_general(
                b_alpha[row_i[k]],
                block_j[k, spans[c]],
                (((1,), (1,)), ((), ())),
                preferred_element_type=jnp.float32,
            )
            half_send[c, :, k] = partial.astype(jnp.bfloat16).reshape(2, half, width)
        halves[c].start()

    def pair_sum(c, k):
        return half_send[c, core, k].astype(jnp.float32) + half_recv[c, k].astype(jnp.float32)

    def crossing(c):
        halves[c].wait_recv()
        for k in each:
            cross_send[c, k] = pair_sum(c, k).astype(jnp.bfloat16)
        for copy in crosses[c]:
            copy.start()

    def amplitude(c):
        for copy in crosses[c]:
            copy.wait_recv()
        gap = vir_column + eps_vir_beta[:, spans[c]]
        for k in each:
            total = pair_sum(c, k)
            for n in hops:
                total = total + cross_recv[c, n, k].astype(jnp.float32)
            occ_alpha = eps_occ_alpha[pair_list[slot[k], 0, owner]]
            occ_beta = eps_occ_beta[pair_list[slot[k], 1, owner]]
            live = live_mask[slot[k], owner].astype(jnp.float32)
            value = live * total / (gap - occ_alpha - occ_beta)
            amp[c, core, k] = value.astype(jnp.bfloat16)
        nears[c].start()

    def terms(c):
        for k in list(away) + list(range(local)):
            term = lax.dot_general(
                amp[c, :, k].reshape(nvir, width),
                b_alpha[row_i[k]],
                (((0,), (0,)), ((), ())),
                preferred_element_type=jnp.float32,
            )
            if k in away:
                term_send[k - local, spans[c]] = term.astype(jnp.bfloat16)
                returns[c][k].start()
            else:
                for r in range(rows):
                    gamma_beta[r, spans[c]] = jnp.where(row_out[k] == r, term, 0.0)

    def finished(c):
        nears[c].wait_recv()
        terms(c)

    for c in steps:
        if c >= 1 and c == chunks - 1:
            finished(0)
        sums(c)
        if c >= 1 and c == chunks - 1:
            for n in steps[1: c - 1]:
                finished(n)
        crossing(c)
        if c >= 1:
            amplitude(c - 1)
    for c in steps[-2:-1]:
        finished(c)
    amplitude(chunks - 1)
    nears[chunks - 1].wait_recv()
    for n in range(parts):
        totals = [jnp.zeros((band, cols), jnp.float32)] * rows
        side, first = divmod(n * band, half)
        for k in each:
            left = jnp.concatenate([amp[c, side, k, pl.ds(first, band)] for c in steps], axis=1)
            term = jnp.dot(left, block_j[k], preferred_element_type=jnp.float32)
            totals = [totals[r] + jnp.where(row_i[k] == r, term, 0.0) for r in range(rows)]
        for r in range(rows):
            if moved:
                sum_send[r, bands[n]] = totals[r].astype(jnp.bfloat16)
            else:
                alpha_sums[r, bands[n]] = totals[r]
        if moved:
            sends[n].start()
    terms(chunks - 1)
    for c in steps:
        for k in away:
            returns[c][k].wait_recv()
        for r in range(rows):
            total = gamma_beta[r, spans[c]] if local else jnp.zeros((width, cols), jnp.float32)
            for k in away:
                total = total + jnp.where(
                    row_out[k] == r, term_recv[k - local, spans[c]].astype(jnp.float32), 0.0
                )
            gamma_beta[r, spans[c]] = total
    for copy in sends:
        copy.wait_recv()
    for copy in alphas + sends:
        copy.wait_send()
    for c in steps:
        for copy in [fetches[c][k] for k in away] + [returns[c][k] for k in away]:
            copy.wait_send()
        for copy in [halves[c], nears[c]] + crosses[c]:
            copy.wait_send()


def write_out(alpha_sums, beta_sums, gamma_alpha, gamma_beta, wide, sems):
    beta = pltpu.make_async_copy(beta_sums, gamma_beta, sems.at[0])
    beta.start()
    copies = [beta]
    for r in range(wide.shape[0]):
        wide[r] = alpha_sums[r].astype(jnp.float32)
        copies.append(pltpu.make_async_copy(wide.at[r], gamma_alpha.at[r], sems.at[1 + r]))
        copies[-1].start()
    for copy in copies:
        copy.wait()


def solution(mesh):
    workers, parts = mesh.shape["occ"], mesh.shape["aux"]

    def shards(
        b_alpha,
        b_beta,
        eps_occ_alpha,
        eps_occ_beta,
        eps_vir_alpha,
        eps_vir_beta,
        row_orbital,
        pair_list,
        live_mask,
    ):
        rows, nvir, cols = b_alpha.shape
        slots = pair_list.shape[0]
        half = nvir // 2
        chips = parts // 2
        vmem = pl.BlockSpec(memory_space=pltpu.VMEM)
        hbm = pl.BlockSpec(memory_space=pltpu.HBM)
        gamma = jax.ShapeDtypeStruct((rows, nvir, cols), jnp.float32)
        moved = workers == 2 * slots
        remote_slots = slots - 1 if moved else slots
        block = pltpu.VMEM((slots, nvir, cols), jnp.bfloat16)
        sent = pltpu.VMEM((remote_slots, nvir, cols), jnp.bfloat16)
        totals = pltpu.VMEM(b_alpha.shape, jnp.bfloat16)
        chunks = max(1, nvir // 128)
        piece = (slots, half, nvir // chunks)
        block_copies = pltpu.SemaphoreType.DMA((2, chunks, remote_slots))
        copies = pltpu.SemaphoreType.DMA((2, chunks))
        hop_copies = pltpu.SemaphoreType.DMA((2, chunks, chips - 1))
        pairs = jnp.transpose(pair_list, (0, 2, 1))
        sums = pl.pallas_call(
            functools.partial(kernel, workers, parts, slots, chunks, moved),
            out_shape=(
                pltpu.VMEM(gamma.shape, jnp.bfloat16 if moved else jnp.float32),
                pltpu.VMEM(gamma.shape, jnp.float32),
            ),
            in_specs=[hbm] * 9,
            out_specs=(vmem, vmem),
            scratch_shapes=[
                pltpu.VMEM(b_alpha.shape, b_alpha.dtype),
                pltpu.VMEM(b_beta.shape, b_beta.dtype),
                pltpu.VMEM((1, nvir), jnp.float32),
                pltpu.VMEM((1, nvir), jnp.float32),
                pltpu.SMEM(eps_occ_alpha.shape, jnp.float32),
                pltpu.SMEM(eps_occ_beta.shape, jnp.float32),
                pltpu.SMEM(row_orbital.shape, jnp.int32),
                pltpu.SMEM(pairs.shape, jnp.int32),
                pltpu.SMEM(live_mask.shape, jnp.int32),
                sent,
                block,
                pltpu.VMEM((chunks, 2) + piece, jnp.bfloat16),
                pltpu.VMEM((chunks,) + piece, jnp.bfloat16),
                pltpu.VMEM((chunks,) + piece, jnp.bfloat16),
                pltpu.VMEM((chunks, chips - 1) + piece, jnp.bfloat16),
                pltpu.VMEM((chunks, 2) + piece, jnp.bfloat16),
                sent,
                sent,
                totals,
                pltpu.SemaphoreType.DMA((9,)),
                block_copies,
                copies,
                hop_copies,
                copies,
                block_copies,
                pltpu.SemaphoreType.DMA((2, rows)),
                pltpu.SemaphoreType.DMA((2, parts)),
            ],
            compiler_params=pltpu.CompilerParams(
                collective_id=0, has_side_effects=True, vmem_limit_bytes=56 * 1024 * 1024
            ),
        )(
            b_alpha,
            b_beta,
            eps_vir_alpha.reshape(1, nvir),
            eps_vir_beta.reshape(1, nvir),
            eps_occ_alpha,
            eps_occ_beta,
            row_orbital,
            pairs,
            live_mask,
        )
        return pl.pallas_call(
            write_out,
            out_shape=(gamma, gamma),
            in_specs=[vmem] * 2,
            out_specs=(hbm, hbm),
            scratch_shapes=[
                pltpu.VMEM(gamma.shape, jnp.float32),
                pltpu.SemaphoreType.DMA((1 + rows,)),
            ],
            compiler_params=pltpu.CompilerParams(vmem_limit_bytes=16 * 1024 * 1024),
        )(*sums)

    placed = (P("occ", None, "aux"), P("occ", None, "aux"), P(), P(), P(), P(), P(), P(), P())
    return jax.shard_map(
        shards,
        mesh=mesh,
        in_specs=placed,
        out_specs=(P("occ", None, "aux"), P("occ", None, "aux")),
        check_vma=False,
    )
```

```python
import functools
import types

import jax
import jax.numpy as jnp
from jax import lax
from jax.experimental import pallas as pl
from jax.experimental.pallas import tpu as pltpu
from jax.sharding import PartitionSpec as P

MESH = pl.DeviceIdType.MESH


def kernel(
    workers,
    parts,
    slots,
    chunks,
    moved,
    b_alpha_hbm,
    b_beta_hbm,
    vir_alpha_hbm,
    vir_beta_hbm,
    occ_alpha_hbm,
    occ_beta_hbm,
    row_orbital_hbm,
    pair_list_hbm,
    live_mask_hbm,
    alpha_sums,
    gamma_beta,
    b_alpha,
    b_beta,
    eps_vir_alpha,
    eps_vir_beta,
    eps_occ_alpha,
    eps_occ_beta,
    row_orbital,
    pair_list,
    live_mask,
    send_block,
    block_j,
    half_send,
    half_recv,
    cross_send,
    cross_recv,
    amp,
    own_half_send,
    own_half_recv,
    own_cross_send,
    own_cross_recv,
    own_amp,
    term_send,
    term_recv,
    sum_send,
    in_sems,
    fetch_sems,
    half_sems,
    cross_sems,
    pair_sems,
    term_sems,
    alpha_sems,
    sum_sems,
):
    rows, nvir, cols = b_alpha.shape
    chips = parts // 2
    half = nvir // 2
    width = nvir // chunks
    worker = lax.axis_index("occ")
    me = lax.axis_index("aux")
    chip, core = me // 2, lax.rem(me, 2)
    partner = me + 1 - 2 * core
    odd = lax.rem(worker, 2)
    turn = 1 - 2 * odd if moved else 0
    if moved:
        place = worker // 2

        def across(k):
            far = place
            for bit in range(k.bit_length()):
                if k >> bit & 1:
                    far = far + 2**bit - 2 ** (bit + 1) * lax.rem(far // 2**bit, 2)
            return far

        ahead = behind = [across(k) * 2 + odd for k in range(slots)]
        slot = [lax.rem(place - across(k) - odd + 2 * slots, slots) for k in range(slots)]
        slot_out = [lax.rem(across(k) - place - odd + 2 * slots, slots) for k in range(slots)]
    else:
        distances = [k * (workers // slots) + 1 for k in range(slots)]
        ahead = [lax.rem(worker + d, workers) for d in distances]
        behind = [lax.rem(worker + workers - d, workers) for d in distances]
        slot = slot_out = range(slots)
    owner = worker + turn
    others = [lax.rem(chip + k, chips) for k in range(1, chips)]

    each = range(slots)
    local = 1 if moved else 0
    away = [k for k in range(2, slots)] + [1] if moved else range(slots)
    hops = range(chips - 1)
    steps = range(chunks)
    spans = [pl.ds(c * width, width) for c in steps]

    loads = [
        pltpu.make_async_copy(src, dst, in_sems.at[n])
        for n, (src, dst) in enumerate(
            [
                (b_beta_hbm, b_beta),
                (row_orbital_hbm, row_orbital),
                (pair_list_hbm, pair_list),
                (live_mask_hbm, live_mask),
                (occ_alpha_hbm, eps_occ_alpha),
                (occ_beta_hbm, eps_occ_beta),
                (vir_alpha_hbm, eps_vir_alpha),
                (vir_beta_hbm, eps_vir_beta),
            ]
            + ([] if moved else [(b_alpha_hbm, b_alpha)])
        )
    ]
    for load in loads:
        load.start()
    barrier = pltpu.get_barrier_semaphore()
    greeted = [ahead[k] for k in away] + ([owner] if moved else [behind[k] for k in away])
    for target in greeted:
        pl.semaphore_signal(barrier, inc=1, device_id={"occ": target}, device_id_type=MESH)
    for peer in [partner] + [other * 2 + core for other in others]:
        pl.semaphore_signal(barrier, inc=1, device_id={"aux": peer}, device_id_type=MESH)
    for load in loads[:3]:
        load.wait()

    def local_row(holder, label):
        found = jnp.int32(0)
        for r in range(rows):
            found = jnp.where(row_orbital[holder * rows + r] == label, r, found)
        return found

    row_i = [local_row(owner, pair_list[slot[k], 0, owner]) for k in each]
    row_out = [local_row(worker, pair_list[slot_out[k], 1, ahead[k] + turn]) for k in each]

    def remote(src, dst, sems, index, where):
        return pltpu.make_async_remote_copy(
            src_ref=src,
            dst_ref=dst,
            send_sem=sems.at[(0,) + index],
            recv_sem=sems.at[(1,) + index],
            device_id=where,
            device_id_type=MESH,
        )

    alphas = [
        remote(b_alpha_hbm.at[r], b_alpha.at[r], alpha_sems, (r,), {"occ": owner})
        for r in range(rows if moved else 0)
    ]
    fetches = [
        {
            k: remote(
                send_block.at[k - local, spans[c]], block_j.at[k, spans[c]], fetch_sems,
                (c, k - local), {"occ": ahead[k]},
            )
            for k in away
        }
        for c in steps
    ]
    def group(n, ids, span, half_out, half_in, cross_out, cross_in, result):
        return types.SimpleNamespace(
            ids=ids,
            span=span,
            half_out=half_out,
            half_in=half_in,
            cross_out=cross_out,
            cross_in=cross_in,
            result=result,
            swap=remote(half_out.at[1 - core], half_in, half_sems, (n,), {"aux": partner}),
            crosses=[
                remote(
                    cross_out, cross_in.at[k], cross_sems, (n, k), {"aux": others[k] * 2 + core}
                )
                for k in hops
            ],
            near=remote(result.at[core], result.at[core], pair_sems, (n,), {"aux": partner}),
        )

    chunked = [
        group(
            c, list(away), spans[c], half_send.at[c], half_recv.at[c], cross_send.at[c],
            cross_recv.at[c], amp.at[c],
        )
        for c in steps
    ]
    own = [
        group(
            chunks + k, [k], pl.ds(0, nvir), own_half_send, own_half_recv, own_cross_send,
            own_cross_recv, own_amp,
        )
        for k in range(local)
    ]
    groups = own + chunked
    returns = [
        {
            k: remote(
                term_send.at[k - local, spans[c]], term_recv.at[k - local, spans[c]], term_sems,
                (c, k - local), {"occ": behind[k]},
            )
            for k in away
        }
        for c in steps
    ]
    band = nvir // parts
    bands = [
        pl.ds(pl.multiple_of((n * band + core * half) % nvir, band), band) for n in range(parts)
    ]
    sends = [
        remote(sum_send.at[:, bands[n]], alpha_sums.at[:, bands[n]], sum_sems, (n,), {"occ": owner})
        for n in range(parts if moved else 0)
    ]

    for k in away:
        send_block[k - local, spans[0]] = b_beta[row_out[k], spans[0]]
    pl.semaphore_wait(barrier, len(greeted) + chips)
    for k in away:
        fetches[0][k].start()
    for copy in alphas:
        copy.start()
    for c in steps[1:]:
        for k in away:
            send_block[k - local, spans[c]] = b_beta[row_out[k], spans[c]]
            fetches[c][k].start()
    for k in range(local):
        block_j[k] = b_beta[row_out[k]]
    for load in loads[3:]:
        load.wait()

    vir_row = eps_vir_alpha[:, pl.ds(pl.multiple_of(core * half, half), half)]
    vir_column = jnp.broadcast_to(vir_row, (128, half)).T[:, :1]
    for copy in alphas:
        copy.wait_recv()

    def sums(g):
        for n, k in enumerate(g.ids):
            if g in chunked:
                fetches[chunked.index(g)][k].wait_recv()
            partial = lax.dot_general(
                b_alpha[row_i[k]],
                block_j[k, g.span],
                (((1,), (1,)), ((), ())),
                preferred_element_type=jnp.float32,
            )
            g.half_out[:, n] = partial.astype(jnp.bfloat16).reshape(2, half, g.span.size)
        g.swap.start()

    def pair_sum(g, n):
        return g.half_out[core, n].astype(jnp.float32) + g.half_in[n].astype(jnp.float32)

    def crossing(g):
        g.swap.wait_recv()
        for n in range(len(g.ids)):
            g.cross_out[n] = pair_sum(g, n).astype(jnp.bfloat16)
        for copy in g.crosses:
            copy.start()

    def amplitude(g):
        for copy in g.crosses:
            copy.wait_recv()
        gap = vir_column + eps_vir_beta[:, g.span]
        for n, k in enumerate(g.ids):
            total = pair_sum(g, n)
            for hop in hops:
                total = total + g.cross_in[hop, n].astype(jnp.float32)
            occ_alpha = eps_occ_alpha[pair_list[slot[k], 0, owner]]
            occ_beta = eps_occ_beta[pair_list[slot[k], 1, owner]]
            live = live_mask[slot[k], owner].astype(jnp.float32)
            value = live * total / (gap - occ_alpha - occ_beta)
            g.result[core, n] = value.astype(jnp.bfloat16)
        g.near.start()

    def terms(g):
        for n, k in enumerate(g.ids):
            term = lax.dot_general(
                g.result[:, n].reshape(nvir, g.span.size),
                b_alpha[row_i[k]],
                (((0,), (0,)), ((), ())),
                preferred_element_type=jnp.float32,
            )
            if g in chunked:
                term_send[k - local, g.span] = term.astype(jnp.bfloat16)
                returns[chunked.index(g)][k].start()
            else:
                for r in range(rows):
                    gamma_beta[r] = jnp.where(row_out[k] == r, term, 0.0)

    def finished(g):
        g.near.wait_recv()
        terms(g)

    last = groups[-1]
    for n, g in enumerate(groups):
        if g is last:
            for ready in own:
                finished(ready)
        sums(g)
        if n >= 2 and groups[n - 2] in chunked:
            finished(groups[n - 2])
        crossing(g)
        if n >= 1:
            amplitude(groups[n - 1])
    for ready in groups[-2:-1]:
        finished(ready)
    amplitude(last)

    for n in range(parts):
        if n == parts // 2:
            last.near.wait_recv()
        side = core if n < parts // 2 else 1 - core
        first = n * band % half
        inside = pl.ds(first, band)
        totals = [jnp.zeros((band, cols), jnp.float32)] * rows
        for k in each:
            if k in away:
                place_k = list(away).index(k)
                left = jnp.concatenate([amp[c, side, place_k, inside] for c in steps], axis=1)
            else:
                left = own_amp[side, 0, inside]
            term = jnp.dot(left, block_j[k], preferred_element_type=jnp.float32)
            totals = [totals[r] + jnp.where(row_i[k] == r, term, 0.0) for r in range(rows)]
        for r in range(rows):
            if moved:
                sum_send[r, bands[n]] = totals[r].astype(jnp.bfloat16)
            else:
                alpha_sums[r, bands[n]] = totals[r]
        if moved:
            sends[n].start()
    terms(last)
    for c in steps:
        for k in away:
            returns[c][k].wait_recv()
        for r in range(rows):
            total = gamma_beta[r, spans[c]] if local else jnp.zeros((width, cols), jnp.float32)
            for k in away:
                total = total + jnp.where(
                    row_out[k] == r, term_recv[k - local, spans[c]].astype(jnp.float32), 0.0
                )
            gamma_beta[r, spans[c]] = total
    for copy in sends:
        copy.wait_recv()
    for copy in alphas + sends:
        copy.wait_send()
    for c in steps:
        for copy in [fetches[c][k] for k in away] + [returns[c][k] for k in away]:
            copy.wait_send()
    for g in groups:
        for copy in [g.swap, g.near] + g.crosses:
            copy.wait_send()


def write_out(alpha_sums, beta_sums, gamma_alpha, gamma_beta, wide, sems):
    beta = pltpu.make_async_copy(beta_sums, gamma_beta, sems.at[0])
    beta.start()
    copies = [beta]
    for r in range(wide.shape[0]):
        wide[r] = alpha_sums[r].astype(jnp.float32)
        copies.append(pltpu.make_async_copy(wide.at[r], gamma_alpha.at[r], sems.at[1 + r]))
        copies[-1].start()
    for copy in copies:
        copy.wait()


def solution(mesh):
    workers, parts = mesh.shape["occ"], mesh.shape["aux"]

    def shards(
        b_alpha,
        b_beta,
        eps_occ_alpha,
        eps_occ_beta,
        eps_vir_alpha,
        eps_vir_beta,
        row_orbital,
        pair_list,
        live_mask,
    ):
        rows, nvir, cols = b_alpha.shape
        slots = pair_list.shape[0]
        half = nvir // 2
        chunks = max(1, nvir // 128)
        moved = workers == 2 * slots and slots & (slots - 1) == 0 and chunks > 1
        chips = parts // 2
        vmem = pl.BlockSpec(memory_space=pltpu.VMEM)
        hbm = pl.BlockSpec(memory_space=pltpu.HBM)
        gamma = jax.ShapeDtypeStruct((rows, nvir, cols), jnp.float32)
        remote_slots = slots - 1 if moved else slots
        block = pltpu.VMEM((slots, nvir, cols), jnp.bfloat16)
        sent = pltpu.VMEM((remote_slots, nvir, cols), jnp.bfloat16)
        totals = pltpu.VMEM(b_alpha.shape, jnp.bfloat16)
        piece = (remote_slots, half, nvir // chunks)
        own = (1, half, nvir)
        block_copies = pltpu.SemaphoreType.DMA((2, chunks, remote_slots))
        copies = pltpu.SemaphoreType.DMA((2, chunks + 1))
        hop_copies = pltpu.SemaphoreType.DMA((2, chunks + 1, chips - 1))
        pairs = jnp.transpose(pair_list, (0, 2, 1))
        sums = pl.pallas_call(
            functools.partial(kernel, workers, parts, slots, chunks, moved),
            out_shape=(
                pltpu.VMEM(gamma.shape, jnp.bfloat16 if moved else jnp.float32),
                pltpu.VMEM(gamma.shape, jnp.float32),
            ),
            in_specs=[hbm] * 9,
            out_specs=(vmem, vmem),
            scratch_shapes=[
                pltpu.VMEM(b_alpha.shape, b_alpha.dtype),
                pltpu.VMEM(b_beta.shape, b_beta.dtype),
                pltpu.VMEM((1, nvir), jnp.float32),
                pltpu.VMEM((1, nvir), jnp.float32),
                pltpu.SMEM(eps_occ_alpha.shape, jnp.float32),
                pltpu.SMEM(eps_occ_beta.shape, jnp.float32),
                pltpu.SMEM(row_orbital.shape, jnp.int32),
                pltpu.SMEM(pairs.shape, jnp.int32),
                pltpu.SMEM(live_mask.shape, jnp.int32),
                sent,
                block,
                pltpu.VMEM((chunks, 2) + piece, jnp.bfloat16),
                pltpu.VMEM((chunks,) + piece, jnp.bfloat16),
                pltpu.VMEM((chunks,) + piece, jnp.bfloat16),
                pltpu.VMEM((chunks, chips - 1) + piece, jnp.bfloat16),
                pltpu.VMEM((chunks, 2) + piece, jnp.bfloat16),
                pltpu.VMEM((2,) + own, jnp.bfloat16),
                pltpu.VMEM(own, jnp.bfloat16),
                pltpu.VMEM(own, jnp.bfloat16),
                pltpu.VMEM((chips - 1,) + own, jnp.bfloat16),
                pltpu.VMEM((2,) + own, jnp.bfloat16),
                sent,
                sent,
                totals,
                pltpu.SemaphoreType.DMA((9,)),
                block_copies,
                copies,
                hop_copies,
                copies,
                block_copies,
                pltpu.SemaphoreType.DMA((2, rows)),
                pltpu.SemaphoreType.DMA((2, parts)),
            ],
            compiler_params=pltpu.CompilerParams(
                collective_id=0, has_side_effects=True, vmem_limit_bytes=56 * 1024 * 1024
            ),
        )(
            b_alpha,
            b_beta,
            eps_vir_alpha.reshape(1, nvir),
            eps_vir_beta.reshape(1, nvir),
            eps_occ_alpha,
            eps_occ_beta,
            row_orbital,
            pairs,
            live_mask,
        )
        return pl.pallas_call(
            write_out,
            out_shape=(gamma, gamma),
            in_specs=[vmem] * 2,
            out_specs=(hbm, hbm),
            scratch_shapes=[
                pltpu.VMEM(gamma.shape, jnp.float32),
                pltpu.SemaphoreType.DMA((1 + rows,)),
            ],
            compiler_params=pltpu.CompilerParams(vmem_limit_bytes=16 * 1024 * 1024),
        )(*sums)

    placed = (P("occ", None, "aux"), P("occ", None, "aux"), P(), P(), P(), P(), P(), P(), P())
    return jax.shard_map(
        shards,
        mesh=mesh,
        in_specs=placed,
        out_specs=(P("occ", None, "aux"), P("occ", None, "aux")),
        check_vma=False,
    )
```

```python
import functools
import types

import jax
import jax.numpy as jnp
from jax import lax
from jax.experimental import pallas as pl
from jax.experimental.pallas import tpu as pltpu
from jax.sharding import PartitionSpec as P

MESH = pl.DeviceIdType.MESH


def kernel(
    workers,
    parts,
    slots,
    chunks,
    moved,
    b_alpha_hbm,
    b_beta_hbm,
    vir_alpha_hbm,
    vir_beta_hbm,
    occ_alpha_hbm,
    occ_beta_hbm,
    row_orbital_hbm,
    pair_list_hbm,
    live_mask_hbm,
    alpha_sums,
    gamma_beta,
    b_alpha,
    b_beta,
    eps_vir_alpha,
    eps_vir_beta,
    eps_occ_alpha,
    eps_occ_beta,
    row_orbital,
    pair_list,
    live_mask,
    send_block,
    block_j,
    half_send,
    half_recv,
    cross_send,
    cross_recv,
    amp,
    own_half_send,
    own_half_recv,
    own_cross_send,
    own_cross_recv,
    own_amp,
    term_send,
    term_recv,
    sum_send,
    in_sems,
    fetch_sems,
    half_sems,
    cross_sems,
    pair_sems,
    term_sems,
    alpha_sems,
    sum_sems,
    ready_sems,
):
    rows, nvir, cols = b_alpha.shape
    chips = parts // 2
    half = nvir // 2
    width = nvir // chunks
    worker = lax.axis_index("occ")
    me = lax.axis_index("aux")
    chip, core = me // 2, lax.rem(me, 2)
    partner = me + 1 - 2 * core
    odd = lax.rem(worker, 2)
    turn = 1 - 2 * odd if moved else 0
    if moved:
        place = worker // 2

        def across(k):
            far = place
            for bit in range(k.bit_length()):
                if k >> bit & 1:
                    far = far + 2**bit - 2 ** (bit + 1) * lax.rem(far // 2**bit, 2)
            return far

        ahead = behind = [across(k) * 2 + odd for k in range(slots)]
        slot = [lax.rem(place - across(k) - odd + 2 * slots, slots) for k in range(slots)]
        slot_out = [lax.rem(across(k) - place - odd + 2 * slots, slots) for k in range(slots)]
    else:
        distances = [k * (workers // slots) + 1 for k in range(slots)]
        ahead = [lax.rem(worker + d, workers) for d in distances]
        behind = [lax.rem(worker + workers - d, workers) for d in distances]
        slot = slot_out = range(slots)
    owner = worker + turn
    others = [lax.rem(chip + k, chips) for k in range(1, chips)]

    each = range(slots)
    local = 1 if moved else 0
    away = [k for k in range(2, slots)] + [1] if moved else range(slots)
    hops = range(chips - 1)
    steps = range(chunks)
    spans = [pl.ds(c * width, width) for c in steps]

    loads = [
        pltpu.make_async_copy(src, dst, in_sems.at[n])
        for n, (src, dst) in enumerate(
            [
                (b_beta_hbm, b_beta),
                (row_orbital_hbm, row_orbital),
                (pair_list_hbm, pair_list),
                (live_mask_hbm, live_mask),
                (occ_alpha_hbm, eps_occ_alpha),
                (occ_beta_hbm, eps_occ_beta),
                (vir_alpha_hbm, eps_vir_alpha),
                (vir_beta_hbm, eps_vir_beta),
            ]
            + ([] if moved else [(b_alpha_hbm, b_alpha)])
        )
    ]
    for load in loads:
        load.start()
    barrier = pltpu.get_barrier_semaphore()
    if moved:
        direct = [k for k in away if k & (k - 1) == 0]
        greeted = [ahead[k] for k in direct] + [owner]
    else:
        direct = away
        greeted = [ahead[k] for k in away] + [behind[k] for k in away]
    for target in greeted:
        pl.semaphore_signal(barrier, inc=1, device_id={"occ": target}, device_id_type=MESH)
    for peer in [partner] + [other * 2 + core for other in others]:
        pl.semaphore_signal(barrier, inc=1, device_id={"aux": peer}, device_id_type=MESH)
    for load in loads[:3]:
        load.wait()

    def local_row(holder, label):
        found = jnp.int32(0)
        for r in range(rows):
            found = jnp.where(row_orbital[holder * rows + r] == label, r, found)
        return found

    row_i = [local_row(owner, pair_list[slot[k], 0, owner]) for k in each]
    row_out = [local_row(worker, pair_list[slot_out[k], 1, ahead[k] + turn]) for k in each]

    def remote(src, dst, sems, index, where):
        return pltpu.make_async_remote_copy(
            src_ref=src,
            dst_ref=dst,
            send_sem=sems.at[(0,) + index],
            recv_sem=sems.at[(1,) + index],
            device_id=where,
            device_id_type=MESH,
        )

    alphas = [
        remote(b_alpha_hbm.at[r], b_alpha.at[r], alpha_sems, (r,), {"occ": owner})
        for r in range(rows if moved else 0)
    ]
    fetches = [
        {
            k: remote(
                send_block.at[k - local, spans[c]], block_j.at[k, spans[c]], fetch_sems,
                (c, k - local), {"occ": ahead[k]},
            )
            for k in away
        }
        for c in steps
    ]
    def group(n, ids, span, half_out, half_in, cross_out, cross_in, result):
        return types.SimpleNamespace(
            ids=ids,
            span=span,
            half_out=half_out,
            half_in=half_in,
            cross_out=cross_out,
            cross_in=cross_in,
            result=result,
            swap=remote(half_out.at[1 - core], half_in, half_sems, (n,), {"aux": partner}),
            crosses=[
                remote(
                    cross_out, cross_in.at[k], cross_sems, (n, k), {"aux": others[k] * 2 + core}
                )
                for k in hops
            ],
            near=remote(result.at[core], result.at[core], pair_sems, (n,), {"aux": partner}),
        )

    chunked = [
        group(
            c, list(away), spans[c], half_send.at[c], half_recv.at[c], cross_send.at[c],
            cross_recv.at[c], amp.at[c],
        )
        for c in steps
    ]
    own = [
        group(
            chunks + k, [k], pl.ds(0, nvir), own_half_send, own_half_recv, own_cross_send,
            own_cross_recv, own_amp,
        )
        for k in range(local)
    ]
    groups = own + chunked
    returns = [
        {
            k: remote(
                term_send.at[k - local, spans[c]], term_recv.at[k - local, spans[c]], term_sems,
                (c, k - local), {"occ": behind[k]},
            )
            for k in away
        }
        for c in steps
    ]
    band = nvir // parts
    bands = [
        pl.ds(pl.multiple_of((n * band + core * half) % nvir, band), band) for n in range(parts)
    ]
    sends = [
        remote(sum_send.at[:, bands[n]], alpha_sums.at[:, bands[n]], sum_sems, (n,), {"occ": owner})
        for n in range(parts if moved else 0)
    ]

    for k in away:
        send_block[k - local, spans[0]] = b_beta[row_out[k], spans[0]]
    pl.semaphore_wait(barrier, len(greeted) + chips)
    relayed = sorted((k for k in away if k not in direct), key=lambda k: k.bit_count())
    entered = list(direct)

    def vouch():
        for k in relayed:
            low = k & -k
            if k not in vouched and k - low in entered:
                vouched.append(k)
                pl.semaphore_signal(
                    ready_sems.at[k], inc=1, device_id={"occ": ahead[low]}, device_id_type=MESH
                )

    vouched = []
    vouch()
    for copy in alphas:
        copy.start()
    for k in direct[:1]:
        fetches[0][k].start()
    for c in steps[1:]:
        for k in away:
            send_block[k - local, spans[c]] = b_beta[row_out[k], spans[c]]
    for k in relayed:
        pl.semaphore_wait(ready_sems.at[k], 1)
        entered.append(k)
        vouch()
        fetches[0][k].start()
    for k in direct[1:]:
        fetches[0][k].start()
    for c in steps[1:]:
        for k in away:
            fetches[c][k].start()
    for k in range(local):
        block_j[k] = b_beta[row_out[k]]
    for load in loads[3:]:
        load.wait()

    vir_row = eps_vir_alpha[:, pl.ds(pl.multiple_of(core * half, half), half)]
    vir_column = jnp.broadcast_to(vir_row, (128, half)).T[:, :1]
    for copy in alphas:
        copy.wait_recv()

    def sums(g):
        for n, k in enumerate(g.ids):
            if g in chunked:
                fetches[chunked.index(g)][k].wait_recv()
            partial = lax.dot_general(
                b_alpha[row_i[k]],
                block_j[k, g.span],
                (((1,), (1,)), ((), ())),
                preferred_element_type=jnp.float32,
            )
            g.half_out[:, n] = partial.astype(jnp.bfloat16).reshape(2, half, g.span.size)
        g.swap.start()

    def pair_sum(g, n):
        return g.half_out[core, n].astype(jnp.float32) + g.half_in[n].astype(jnp.float32)

    def crossing(g):
        g.swap.wait_recv()
        for n in range(len(g.ids)):
            g.cross_out[n] = pair_sum(g, n).astype(jnp.bfloat16)
        for copy in g.crosses:
            copy.start()

    def amplitude(g):
        for copy in g.crosses:
            copy.wait_recv()
        gap = vir_column + eps_vir_beta[:, g.span]
        for n, k in enumerate(g.ids):
            total = pair_sum(g, n)
            for hop in hops:
                total = total + g.cross_in[hop, n].astype(jnp.float32)
            occ_alpha = eps_occ_alpha[pair_list[slot[k], 0, owner]]
            occ_beta = eps_occ_beta[pair_list[slot[k], 1, owner]]
            live = live_mask[slot[k], owner].astype(jnp.float32)
            value = live * total / (gap - occ_alpha - occ_beta)
            g.result[core, n] = value.astype(jnp.bfloat16)
        g.near.start()

    def terms(g):
        for n, k in enumerate(g.ids):
            term = lax.dot_general(
                g.result[:, n].reshape(nvir, g.span.size),
                b_alpha[row_i[k]],
                (((0,), (0,)), ((), ())),
                preferred_element_type=jnp.float32,
            )
            if g in chunked:
                term_send[k - local, g.span] = term.astype(jnp.bfloat16)
                returns[chunked.index(g)][k].start()
            else:
                for r in range(rows):
                    gamma_beta[r] = jnp.where(row_out[k] == r, term, 0.0)

    def finished(g):
        g.near.wait_recv()
        terms(g)

    last = groups[-1]
    for n, g in enumerate(groups):
        if n >= 2 and groups[n - 2] in chunked:
            finished(groups[n - 2])
        sums(g)
        crossing(g)
        if n >= 1:
            amplitude(groups[n - 1])
    for ready in groups[-2:-1]:
        finished(ready)
    amplitude(last)
    for ready in own:
        ready.near.wait_recv()

    for n in range(parts):
        if n == parts // 2:
            last.near.wait_recv()
        side = core if n < parts // 2 else 1 - core
        first = n * band % half
        inside = pl.ds(first, band)
        totals = [jnp.zeros((band, cols), jnp.float32)] * rows
        for k in each:
            if k in away:
                place_k = list(away).index(k)
                left = jnp.concatenate([amp[c, side, place_k, inside] for c in steps], axis=1)
            else:
                left = own_amp[side, 0, inside]
            term = jnp.dot(left, block_j[k], preferred_element_type=jnp.float32)
            totals = [totals[r] + jnp.where(row_i[k] == r, term, 0.0) for r in range(rows)]
        for r in range(rows):
            if moved:
                sum_send[r, bands[n]] = totals[r].astype(jnp.bfloat16)
            else:
                alpha_sums[r, bands[n]] = totals[r]
        if moved:
            sends[n].start()
    terms(last)
    for ready in own:
        terms(ready)
    for c in steps:
        for k in away:
            returns[c][k].wait_recv()
        for r in range(rows):
            total = gamma_beta[r, spans[c]] if local else jnp.zeros((width, cols), jnp.float32)
            for k in away:
                total = total + jnp.where(
                    row_out[k] == r, term_recv[k - local, spans[c]].astype(jnp.float32), 0.0
                )
            gamma_beta[r, spans[c]] = total
    for copy in sends:
        copy.wait_recv()
    for copy in alphas + sends:
        copy.wait_send()
    for c in steps:
        for copy in [fetches[c][k] for k in away] + [returns[c][k] for k in away]:
            copy.wait_send()
    for g in groups:
        for copy in [g.swap, g.near] + g.crosses:
            copy.wait_send()


def write_out(alpha_sums, beta_sums, gamma_alpha, gamma_beta, wide, sems):
    beta = pltpu.make_async_copy(beta_sums, gamma_beta, sems.at[0])
    beta.start()
    copies = [beta]
    for r in range(wide.shape[0]):
        wide[r] = alpha_sums[r].astype(jnp.float32)
        copies.append(pltpu.make_async_copy(wide.at[r], gamma_alpha.at[r], sems.at[1 + r]))
        copies[-1].start()
    for copy in copies:
        copy.wait()


def solution(mesh):
    workers, parts = mesh.shape["occ"], mesh.shape["aux"]

    def shards(
        b_alpha,
        b_beta,
        eps_occ_alpha,
        eps_occ_beta,
        eps_vir_alpha,
        eps_vir_beta,
        row_orbital,
        pair_list,
        live_mask,
    ):
        rows, nvir, cols = b_alpha.shape
        slots = pair_list.shape[0]
        half = nvir // 2
        chunks = max(1, nvir // 128)
        moved = workers == 2 * slots and slots & (slots - 1) == 0 and chunks > 1
        chips = parts // 2
        vmem = pl.BlockSpec(memory_space=pltpu.VMEM)
        hbm = pl.BlockSpec(memory_space=pltpu.HBM)
        gamma = jax.ShapeDtypeStruct((rows, nvir, cols), jnp.float32)
        remote_slots = slots - 1 if moved else slots
        block = pltpu.VMEM((slots, nvir, cols), jnp.bfloat16)
        sent = pltpu.VMEM((remote_slots, nvir, cols), jnp.bfloat16)
        totals = pltpu.VMEM(b_alpha.shape, jnp.bfloat16)
        piece = (remote_slots, half, nvir // chunks)
        own = (1, half, nvir)
        block_copies = pltpu.SemaphoreType.DMA((2, chunks, remote_slots))
        copies = pltpu.SemaphoreType.DMA((2, chunks + 1))
        hop_copies = pltpu.SemaphoreType.DMA((2, chunks + 1, chips - 1))
        pairs = jnp.transpose(pair_list, (0, 2, 1))
        sums = pl.pallas_call(
            functools.partial(kernel, workers, parts, slots, chunks, moved),
            out_shape=(
                pltpu.VMEM(gamma.shape, jnp.bfloat16 if moved else jnp.float32),
                pltpu.VMEM(gamma.shape, jnp.float32),
            ),
            in_specs=[hbm] * 9,
            out_specs=(vmem, vmem),
            scratch_shapes=[
                pltpu.VMEM(b_alpha.shape, b_alpha.dtype),
                pltpu.VMEM(b_beta.shape, b_beta.dtype),
                pltpu.VMEM((1, nvir), jnp.float32),
                pltpu.VMEM((1, nvir), jnp.float32),
                pltpu.SMEM(eps_occ_alpha.shape, jnp.float32),
                pltpu.SMEM(eps_occ_beta.shape, jnp.float32),
                pltpu.SMEM(row_orbital.shape, jnp.int32),
                pltpu.SMEM(pairs.shape, jnp.int32),
                pltpu.SMEM(live_mask.shape, jnp.int32),
                sent,
                block,
                pltpu.VMEM((chunks, 2) + piece, jnp.bfloat16),
                pltpu.VMEM((chunks,) + piece, jnp.bfloat16),
                pltpu.VMEM((chunks,) + piece, jnp.bfloat16),
                pltpu.VMEM((chunks, chips - 1) + piece, jnp.bfloat16),
                pltpu.VMEM((chunks, 2) + piece, jnp.bfloat16),
                pltpu.VMEM((2,) + own, jnp.bfloat16),
                pltpu.VMEM(own, jnp.bfloat16),
                pltpu.VMEM(own, jnp.bfloat16),
                pltpu.VMEM((chips - 1,) + own, jnp.bfloat16),
                pltpu.VMEM((2,) + own, jnp.bfloat16),
                sent,
                sent,
                totals,
                pltpu.SemaphoreType.DMA((9,)),
                block_copies,
                copies,
                hop_copies,
                copies,
                block_copies,
                pltpu.SemaphoreType.DMA((2, rows)),
                pltpu.SemaphoreType.DMA((2, parts)),
                pltpu.SemaphoreType.REGULAR((slots,)),
            ],
            compiler_params=pltpu.CompilerParams(
                collective_id=0, has_side_effects=True, vmem_limit_bytes=56 * 1024 * 1024
            ),
        )(
            b_alpha,
            b_beta,
            eps_vir_alpha.reshape(1, nvir),
            eps_vir_beta.reshape(1, nvir),
            eps_occ_alpha,
            eps_occ_beta,
            row_orbital,
            pairs,
            live_mask,
        )
        return pl.pallas_call(
            write_out,
            out_shape=(gamma, gamma),
            in_specs=[vmem] * 2,
            out_specs=(hbm, hbm),
            scratch_shapes=[
                pltpu.VMEM(gamma.shape, jnp.float32),
                pltpu.SemaphoreType.DMA((1 + rows,)),
            ],
            compiler_params=pltpu.CompilerParams(vmem_limit_bytes=16 * 1024 * 1024),
        )(*sums)

    placed = (P("occ", None, "aux"), P("occ", None, "aux"), P(), P(), P(), P(), P(), P(), P())
    return jax.shard_map(
        shards,
        mesh=mesh,
        in_specs=placed,
        out_specs=(P("occ", None, "aux"), P("occ", None, "aux")),
        check_vma=False,
    )
```

```python
import functools
import types

import jax
import jax.numpy as jnp
from jax import lax
from jax.experimental import pallas as pl
from jax.experimental.pallas import tpu as pltpu
from jax.sharding import PartitionSpec as P

MESH = pl.DeviceIdType.MESH


def kernel(
    workers,
    parts,
    slots,
    chunks,
    moved,
    b_alpha_hbm,
    b_beta_hbm,
    vir_alpha_hbm,
    vir_beta_hbm,
    occ_alpha_hbm,
    occ_beta_hbm,
    row_orbital_hbm,
    pair_list_hbm,
    live_mask_hbm,
    alpha_sums,
    gamma_beta,
    b_alpha,
    b_beta,
    eps_vir_alpha,
    eps_vir_beta,
    eps_occ_alpha,
    eps_occ_beta,
    row_orbital,
    pair_list,
    live_mask,
    send_block,
    block_j,
    half_send,
    half_recv,
    cross_send,
    cross_recv,
    amp,
    own_half_send,
    own_half_recv,
    own_cross_send,
    own_cross_recv,
    own_amp,
    term_send,
    term_recv,
    sum_send,
    sum_recv,
    in_sems,
    fetch_sems,
    half_sems,
    cross_sems,
    pair_sems,
    term_sems,
    alpha_sems,
    sum_sems,
    ready_sems,
):
    rows, nvir, cols = b_alpha.shape
    chips = parts // 2
    half = nvir // 2
    width = nvir // chunks
    worker = lax.axis_index("occ")
    me = lax.axis_index("aux")
    chip, core = me // 2, lax.rem(me, 2)
    partner = me + 1 - 2 * core
    odd = lax.rem(worker, 2)
    turn = 1 - 2 * odd if moved else 0
    if moved:
        place = worker // 2

        def across(k):
            far = place
            for bit in range(k.bit_length()):
                if k >> bit & 1:
                    far = far + 2**bit - 2 ** (bit + 1) * lax.rem(far // 2**bit, 2)
            return far

        ahead = behind = [across(k) * 2 + odd for k in range(slots)]
        slot = [lax.rem(place - across(k) - odd + 2 * slots, slots) for k in range(slots)]
        slot_out = [lax.rem(across(k) - place - odd + 2 * slots, slots) for k in range(slots)]
    else:
        distances = [k * (workers // slots) + 1 for k in range(slots)]
        ahead = [lax.rem(worker + d, workers) for d in distances]
        behind = [lax.rem(worker + workers - d, workers) for d in distances]
        slot = slot_out = range(slots)
    owner = worker + turn
    others = [lax.rem(chip + k, chips) for k in range(1, chips)]

    each = range(slots)
    local = 1 if moved else 0
    away = [k for k in range(2, slots)] + [1] if moved else range(slots)
    hops = range(chips - 1)
    steps = range(chunks)
    spans = [pl.ds(c * width, width) for c in steps]

    loads = [
        pltpu.make_async_copy(src, dst, in_sems.at[n])
        for n, (src, dst) in enumerate(
            [
                (b_beta_hbm, b_beta),
                (row_orbital_hbm, row_orbital),
                (pair_list_hbm, pair_list),
                (live_mask_hbm, live_mask),
                (occ_alpha_hbm, eps_occ_alpha),
                (occ_beta_hbm, eps_occ_beta),
                (vir_alpha_hbm, eps_vir_alpha),
                (vir_beta_hbm, eps_vir_beta),
            ]
            + ([] if moved else [(b_alpha_hbm, b_alpha)])
        )
    ]
    for load in loads:
        load.start()
    barrier = pltpu.get_barrier_semaphore()
    if moved:
        direct = [k for k in away if k & (k - 1) == 0]
        greeted = [ahead[k] for k in direct] + [owner]
    else:
        direct = away
        greeted = [ahead[k] for k in away] + [behind[k] for k in away]
    for target in greeted:
        pl.semaphore_signal(barrier, inc=1, device_id={"occ": target}, device_id_type=MESH)
    for peer in [partner] + [other * 2 + core for other in others]:
        pl.semaphore_signal(barrier, inc=1, device_id={"aux": peer}, device_id_type=MESH)
    for load in loads[:3]:
        load.wait()

    def local_row(holder, label):
        found = jnp.int32(0)
        for r in range(rows):
            found = jnp.where(row_orbital[holder * rows + r] == label, r, found)
        return found

    row_i = [local_row(owner, pair_list[slot[k], 0, owner]) for k in each]
    row_out = [local_row(worker, pair_list[slot_out[k], 1, ahead[k] + turn]) for k in each]

    def remote(src, dst, sems, index, where):
        return pltpu.make_async_remote_copy(
            src_ref=src,
            dst_ref=dst,
            send_sem=sems.at[(0,) + index],
            recv_sem=sems.at[(1,) + index],
            device_id=where,
            device_id_type=MESH,
        )

    alphas = [
        remote(b_alpha_hbm.at[r], b_alpha.at[r], alpha_sems, (r,), {"occ": owner})
        for r in range(rows if moved else 0)
    ]
    fetches = [
        {
            k: remote(
                send_block.at[k - local, spans[c]], block_j.at[k, spans[c]], fetch_sems,
                (c, k - local), {"occ": ahead[k]},
            )
            for k in away
        }
        for c in steps
    ]
    def group(n, ids, span, half_out, half_in, cross_out, cross_in, result):
        return types.SimpleNamespace(
            ids=ids,
            span=span,
            half_out=half_out,
            half_in=half_in,
            cross_out=cross_out,
            cross_in=cross_in,
            result=result,
            swap=remote(half_out.at[1 - core], half_in, half_sems, (n,), {"aux": partner}),
            crosses=[
                remote(
                    cross_out, cross_in.at[k], cross_sems, (n, k), {"aux": others[k] * 2 + core}
                )
                for k in hops
            ],
            near=remote(result.at[core], result.at[core], pair_sems, (n,), {"aux": partner}),
        )

    chunked = [
        group(
            c, list(away), spans[c], half_send.at[c], half_recv.at[c], cross_send.at[c],
            cross_recv.at[c], amp.at[c],
        )
        for c in steps
    ]
    own = [
        group(
            chunks + k, [k], pl.ds(0, nvir), own_half_send, own_half_recv, own_cross_send,
            own_cross_recv, own_amp,
        )
        for k in range(local)
    ]
    groups = own + chunked
    returns = [
        {
            k: remote(
                term_send.at[k - local, spans[c]], term_recv.at[k - local, spans[c]], term_sems,
                (c, k - local), {"occ": behind[k]},
            )
            for k in away
        }
        for c in steps
    ]
    band = nvir // parts
    bands = [
        pl.ds(pl.multiple_of((n * band + core * half) % nvir, band), band) for n in range(parts)
    ]
    sends = [
        remote(sum_send.at[:, bands[n]], sum_recv.at[:, bands[n]], sum_sems, (n,), {"occ": owner})
        for n in range(parts if moved else 0)
    ]

    for k in away:
        send_block[k - local, spans[0]] = b_beta[row_out[k], spans[0]]
    pl.semaphore_wait(barrier, len(greeted) + chips)
    relayed = sorted((k for k in away if k not in direct), key=lambda k: k.bit_count())
    entered = list(direct)

    def vouch():
        for k in relayed:
            low = k & -k
            if k not in vouched and k - low in entered:
                vouched.append(k)
                pl.semaphore_signal(
                    ready_sems.at[k], inc=1, device_id={"occ": ahead[low]}, device_id_type=MESH
                )

    vouched = []
    vouch()
    for copy in alphas:
        copy.start()
    for k in direct[:1]:
        fetches[0][k].start()
    for c in steps[1:]:
        for k in away:
            send_block[k - local, spans[c]] = b_beta[row_out[k], spans[c]]
    for k in relayed:
        pl.semaphore_wait(ready_sems.at[k], 1)
        entered.append(k)
        vouch()
        fetches[0][k].start()
    for k in direct[1:]:
        fetches[0][k].start()
    for c in steps[1:]:
        for k in away:
            fetches[c][k].start()
    for k in range(local):
        block_j[k] = b_beta[row_out[k]]
    for load in loads[3:]:
        load.wait()

    vir_row = eps_vir_alpha[:, pl.ds(pl.multiple_of(core * half, half), half)]
    vir_column = jnp.broadcast_to(vir_row, (128, half)).T[:, :1]
    for copy in alphas:
        copy.wait_recv()

    def sums(g):
        for n, k in enumerate(g.ids):
            if g in chunked:
                fetches[chunked.index(g)][k].wait_recv()
            partial = lax.dot_general(
                b_alpha[row_i[k]],
                block_j[k, g.span],
                (((1,), (1,)), ((), ())),
                preferred_element_type=jnp.float32,
            )
            g.half_out[:, n] = partial.astype(jnp.bfloat16).reshape(2, half, g.span.size)
        g.swap.start()

    def pair_sum(g, n):
        return g.half_out[core, n].astype(jnp.float32) + g.half_in[n].astype(jnp.float32)

    def crossing(g):
        g.swap.wait_recv()
        for n in range(len(g.ids)):
            g.cross_out[n] = pair_sum(g, n).astype(jnp.bfloat16)
        for copy in g.crosses:
            copy.start()

    def amplitude(g):
        for copy in g.crosses:
            copy.wait_recv()
        gap = vir_column + eps_vir_beta[:, g.span]
        for n, k in enumerate(g.ids):
            total = pair_sum(g, n)
            for hop in hops:
                total = total + g.cross_in[hop, n].astype(jnp.float32)
            occ_alpha = eps_occ_alpha[pair_list[slot[k], 0, owner]]
            occ_beta = eps_occ_beta[pair_list[slot[k], 1, owner]]
            live = live_mask[slot[k], owner].astype(jnp.float32)
            value = live * total / (gap - occ_alpha - occ_beta)
            g.result[core, n] = value.astype(jnp.bfloat16)
        g.near.start()

    def terms(g):
        for n, k in enumerate(g.ids):
            term = lax.dot_general(
                g.result[:, n].reshape(nvir, g.span.size),
                b_alpha[row_i[k]],
                (((0,), (0,)), ((), ())),
                preferred_element_type=jnp.float32,
            )
            if g in chunked:
                term_send[k - local, g.span] = term.astype(jnp.bfloat16)
                returns[chunked.index(g)][k].start()
            else:
                for r in range(rows):
                    gamma_beta[r] = jnp.where(row_out[k] == r, term, 0.0)

    def finished(g):
        g.near.wait_recv()
        terms(g)

    last = groups[-1]
    for n, g in enumerate(groups):
        if n >= 2 and groups[n - 2] in chunked:
            finished(groups[n - 2])
        sums(g)
        crossing(g)
        if n >= 1:
            amplitude(groups[n - 1])
    for ready in groups[-2:-1]:
        finished(ready)
    amplitude(last)
    for ready in own:
        ready.near.wait_recv()

    for n in range(parts):
        if n == parts // 2:
            last.near.wait_recv()
        side = core if n < parts // 2 else 1 - core
        first = n * band % half
        inside = pl.ds(first, band)
        totals = [jnp.zeros((band, cols), jnp.float32)] * rows
        for k in each:
            if k in away:
                place_k = list(away).index(k)
                left = jnp.concatenate([amp[c, side, place_k, inside] for c in steps], axis=1)
            else:
                left = own_amp[side, 0, inside]
            term = jnp.dot(left, block_j[k], preferred_element_type=jnp.float32)
            totals = [totals[r] + jnp.where(row_i[k] == r, term, 0.0) for r in range(rows)]
        for r in range(rows):
            if moved:
                sum_send[r, bands[n]] = totals[r].astype(jnp.bfloat16)
            else:
                alpha_sums[r, bands[n]] = totals[r]
        if moved:
            sends[n].start()
    terms(last)
    for ready in own:
        terms(ready)
    def collect(c):
        for k in away:
            returns[c][k].wait_recv()
        for r in range(rows):
            total = gamma_beta[r, spans[c]] if local else jnp.zeros((width, cols), jnp.float32)
            for k in away:
                total = total + jnp.where(
                    row_out[k] == r, term_recv[k - local, spans[c]].astype(jnp.float32), 0.0
                )
            gamma_beta[r, spans[c]] = total

    for c in steps[:-1]:
        collect(c)
    for copy in sends:
        copy.wait_recv()
    if moved:
        for r in range(rows):
            alpha_sums[r] = sum_recv[r].astype(jnp.float32)
    collect(chunks - 1)
    for copy in alphas + sends:
        copy.wait_send()
    for c in steps:
        for copy in [fetches[c][k] for k in away] + [returns[c][k] for k in away]:
            copy.wait_send()
    for g in groups:
        for copy in [g.swap, g.near] + g.crosses:
            copy.wait_send()


def write_out(alpha_sums, beta_sums, gamma_alpha, gamma_beta, sems):
    copies = [
        pltpu.make_async_copy(alpha_sums, gamma_alpha, sems.at[0]),
        pltpu.make_async_copy(beta_sums, gamma_beta, sems.at[1]),
    ]
    for copy in copies:
        copy.start()
    for copy in copies:
        copy.wait()


def solution(mesh):
    workers, parts = mesh.shape["occ"], mesh.shape["aux"]

    def shards(
        b_alpha,
        b_beta,
        eps_occ_alpha,
        eps_occ_beta,
        eps_vir_alpha,
        eps_vir_beta,
        row_orbital,
        pair_list,
        live_mask,
    ):
        rows, nvir, cols = b_alpha.shape
        slots = pair_list.shape[0]
        half = nvir // 2
        chunks = max(1, nvir // 128)
        moved = workers == 2 * slots and slots & (slots - 1) == 0 and chunks > 1
        chips = parts // 2
        vmem = pl.BlockSpec(memory_space=pltpu.VMEM)
        hbm = pl.BlockSpec(memory_space=pltpu.HBM)
        gamma = jax.ShapeDtypeStruct((rows, nvir, cols), jnp.float32)
        remote_slots = slots - 1 if moved else slots
        block = pltpu.VMEM((slots, nvir, cols), jnp.bfloat16)
        sent = pltpu.VMEM((remote_slots, nvir, cols), jnp.bfloat16)
        totals = pltpu.VMEM(b_alpha.shape, jnp.bfloat16)
        piece = (remote_slots, half, nvir // chunks)
        own = (1, half, nvir)
        block_copies = pltpu.SemaphoreType.DMA((2, chunks, remote_slots))
        copies = pltpu.SemaphoreType.DMA((2, chunks + 1))
        hop_copies = pltpu.SemaphoreType.DMA((2, chunks + 1, chips - 1))
        pairs = jnp.transpose(pair_list, (0, 2, 1))
        sums = pl.pallas_call(
            functools.partial(kernel, workers, parts, slots, chunks, moved),
            out_shape=(
                pltpu.VMEM(gamma.shape, jnp.float32),
                pltpu.VMEM(gamma.shape, jnp.float32),
            ),
            in_specs=[hbm] * 9,
            out_specs=(vmem, vmem),
            scratch_shapes=[
                pltpu.VMEM(b_alpha.shape, b_alpha.dtype),
                pltpu.VMEM(b_beta.shape, b_beta.dtype),
                pltpu.VMEM((1, nvir), jnp.float32),
                pltpu.VMEM((1, nvir), jnp.float32),
                pltpu.SMEM(eps_occ_alpha.shape, jnp.float32),
                pltpu.SMEM(eps_occ_beta.shape, jnp.float32),
                pltpu.SMEM(row_orbital.shape, jnp.int32),
                pltpu.SMEM(pairs.shape, jnp.int32),
                pltpu.SMEM(live_mask.shape, jnp.int32),
                sent,
                block,
                pltpu.VMEM((chunks, 2) + piece, jnp.bfloat16),
                pltpu.VMEM((chunks,) + piece, jnp.bfloat16),
                pltpu.VMEM((chunks,) + piece, jnp.bfloat16),
                pltpu.VMEM((chunks, chips - 1) + piece, jnp.bfloat16),
                pltpu.VMEM((chunks, 2) + piece, jnp.bfloat16),
                pltpu.VMEM((2,) + own, jnp.bfloat16),
                pltpu.VMEM(own, jnp.bfloat16),
                pltpu.VMEM(own, jnp.bfloat16),
                pltpu.VMEM((chips - 1,) + own, jnp.bfloat16),
                pltpu.VMEM((2,) + own, jnp.bfloat16),
                sent,
                sent,
                totals,
                totals,
                pltpu.SemaphoreType.DMA((9,)),
                block_copies,
                copies,
                hop_copies,
                copies,
                block_copies,
                pltpu.SemaphoreType.DMA((2, rows)),
                pltpu.SemaphoreType.DMA((2, parts)),
                pltpu.SemaphoreType.REGULAR((slots,)),
            ],
            compiler_params=pltpu.CompilerParams(
                collective_id=0, has_side_effects=True, vmem_limit_bytes=56 * 1024 * 1024
            ),
        )(
            b_alpha,
            b_beta,
            eps_vir_alpha.reshape(1, nvir),
            eps_vir_beta.reshape(1, nvir),
            eps_occ_alpha,
            eps_occ_beta,
            row_orbital,
            pairs,
            live_mask,
        )
        return pl.pallas_call(
            write_out,
            out_shape=(gamma, gamma),
            in_specs=[vmem] * 2,
            out_specs=(hbm, hbm),
            scratch_shapes=[
                pltpu.SemaphoreType.DMA((2,)),
            ],
            compiler_params=pltpu.CompilerParams(vmem_limit_bytes=16 * 1024 * 1024),
        )(*sums)

    placed = (P("occ", None, "aux"), P("occ", None, "aux"), P(), P(), P(), P(), P(), P(), P())
    return jax.shard_map(
        shards,
        mesh=mesh,
        in_specs=placed,
        out_specs=(P("occ", None, "aux"), P("occ", None, "aux")),
        check_vma=False,
    )
```
